32 devices in a mesh: row: 8 (over z, y), col: 4 (over x, core).
Axes of the slice: x: 2, y: 2, z: 4, core: 2. Of those that a mesh axis runs over, the one named last changes fastest.
Arguments:
- amplitudes: float32 [8, 8, 384, 384], P('row', 'col'), may hold values from -6 to 6
- exchange_ints: float32 [8, 8, 384, 384], P('row', 'col'), may hold values from -6 to 6
- virt_fock: float32 [384, 384], replicated, as said below
- intersection: float32 [384, 384], replicated, as said below
- occ_fock: float32 [8, 8], replicated, may hold values from -1.5 to 0.3, as said below
- virt_energy: float32 [384], replicated, may hold values from 1 to 3
- fock_tiles: int32 [3, 3], replicated, may hold values from 0 to 1, as said below
- intersection_tiles: int32 [3, 3], replicated, may hold values from 0 to 1, as said below
- occ_pattern: int32 [8, 8], replicated, may hold values from 0 to 1, as said below
- pair_domain: int32 [8, 8, 3], P('row', 'col'), may hold values 0 or 1
Outputs:
- new_amplitudes: float32 [8, 8, 384, 384], P('row', 'col')
The draws below stay inside these ranges and needn't reach their ends.
Inputs may be any that keep to these rules, and one draw needn't show every extreme that they name: `virt_fock`: symmetric. `intersection`: symmetric. `occ_fock`: diagonal entries between -1.5 and -0.3, the others between -0.3 and 0.3. `fock_tiles`: symmetric, every diagonal tile 1, some off-diagonal tile 0. `intersection_tiles`: symmetric, every diagonal tile 1, some off-diagonal tile 0. `occ_pattern`: 1 on the diagonal, 0 where the two orbitals lie more than 1 apart in index.
All inputs are finite; a program needn't handle non-finite values. No bound on the sum of `pair_domain` on one device may be relied on, other than what follows from the above.
Results may differ from the reference program's by a relative error of at most 0.0001.
Values sent between devices are 32-bit elements; how exact they have to be, the bound alone decides.
No kernel may reach another device: no remote copies, remote signals or barrier semaphores. Data moves between devices by JAX's collectives and lax.ppermute only.
A program may use at most 64 MiB of HBM per device.

```python
import math
import jax
import jax.numpy as jnp
from jax import lax

NV = 384
TILE = 128
BAND = 1
ITERS = 2
NO = 8
NT = 3


def symmetric_part(key, spread):
    random_mat = jax.random.normal(key, (NV, NV), jnp.float32)
    return (random_mat + random_mat.T) * (spread / math.sqrt(2.0 * NV))


def draw_virt_fock(key, part):
    key_off, key_diag = jax.random.split(jax.random.fold_in(key, 11))
    off_part = symmetric_part(key_off, 0.5)
    diagonal = jax.random.uniform(key_diag, (NV,), jnp.float32, 1.0, 3.0)
    return off_part + jnp.diag(diagonal)


def draw_intersection(key, part):
    key_off = jax.random.fold_in(key, 23)
    off_part = symmetric_part(key_off, 0.3)
    return off_part + jnp.eye(NV, dtype=jnp.float32)


def draw_occ_fock(key, part):
    key_off, key_diag = jax.random.split(jax.random.fold_in(key, 37))
    off_part = jax.random.uniform(key_off, (NO, NO), jnp.float32, -0.3, 0.3)
    diagonal = jax.random.uniform(key_diag, (NO,), jnp.float32, -1.5, -0.3)
    return jnp.where(jnp.eye(NO, dtype=bool), jnp.diag(diagonal), off_part)


def symmetric_tiles(key):
    key_bits, key_first, key_step = jax.random.split(key, 3)
    random_bits = jax.random.randint(key_bits, (NT, NT), 0, 2)
    positions = jnp.arange(NT)
    upper = positions[:, None] < positions[None, :]
    joined = jnp.where(upper, random_bits, random_bits.T)
    first_tile = jax.random.randint(key_first, (), 0, NT)
    other_tile = (first_tile + jax.random.randint(key_step, (), 1, NT)) % NT
    cleared = (positions[:, None] == first_tile) & (positions[None, :] == other_tile) | (positions[:, None] == other_tile) & (positions[None, :] == first_tile)
    joined = jnp.where(cleared, 0, joined)
    return jnp.where(jnp.eye(NT, dtype=bool), 1, joined).astype(jnp.int32)


def draw_fock_tiles(key, part):
    return symmetric_tiles(jax.random.fold_in(key, 41))


def draw_intersection_tiles(key, part):
    return symmetric_tiles(jax.random.fold_in(key, 43))


def draw_occ_pattern(key, part):
    random_bits = jax.random.randint(jax.random.fold_in(key, 47), (NO, NO), 0, 2)
    positions = jnp.arange(NO)
    distance = jnp.abs(positions[:, None] - positions[None, :])
    return jnp.where(distance == 0, 1, jnp.where(distance <= BAND, random_bits, 0)).astype(jnp.int32)


def plant(entries, key, least, high):
    spot = [jax.random.randint(jax.random.fold_in(key, axis), (), 0, length) for axis, length in enumerate(entries.shape)]
    widest = entries.shape.index(max(entries.shape))
    neighbour = spot[:widest] + [(spot[widest] + 1) % entries.shape[widest]] + spot[widest + 1:]
    return entries.at[tuple(spot)].set(least).at[tuple(neighbour)].set(high)


def block_scale(key, extent, cuts, least, largest):
    level, own = 1.0, jax.random.fold_in(key, 6)
    for dim, shards_of in cuts:
        draws = jnp.exp(jax.random.uniform(jax.random.fold_in(own, dim), (shards_of,), jnp.float32, least / len(cuts), largest / len(cuts)))
        level = level * jnp.repeat(draws, extent[dim] // shards_of).reshape([-1 if axis == dim else 1 for axis in range(len(extent))])
    return level


def normal_values(key, extent, deviation, limit, shards=(), kind=jnp.bfloat16):
    entries = jax.random.normal(key, extent, jnp.float32) * deviation
    if len(shards) > 0:
        entries = block_scale(key, extent, shards, -0.22, 0.18) * entries
    return jnp.clip(entries, min=-limit, max=limit).astype(kind)


def setup_inputs(seed: int = 0) -> dict:
    seeds = jax.random.split(jax.random.key(seed), 11)
    amplitudes = normal_values(seeds[0], (NO, NO, NV, NV), 1.0, 6.0, ((0, 8), (1, 4)), jnp.float32)
    exchange_ints = normal_values(seeds[1], (NO, NO, NV, NV), 1.0, 6.0, ((0, 8), (1, 4)), jnp.float32)
    virt_fock = draw_virt_fock(jax.random.fold_in(seeds[10], 71), 0)
    intersection = draw_intersection(jax.random.fold_in(seeds[10], 71), 0)
    occ_fock = draw_occ_fock(jax.random.fold_in(seeds[10], 71), 0)
    virt_energy = jnp.clip(jax.random.uniform(seeds[5], (NV,), jnp.float32, 1.0, 3.0), 1.0, 3.0)
    fock_tiles = draw_fock_tiles(jax.random.fold_in(seeds[10], 71), 0)
    intersection_tiles = draw_intersection_tiles(jax.random.fold_in(seeds[10], 71), 0)
    occ_pattern = draw_occ_pattern(jax.random.fold_in(seeds[10], 71), 0)
    pair_domain = plant((jax.random.randint(seeds[9], (NO, NO, NT), 0, 4) < 3).astype(jnp.int32), jax.random.fold_in(seeds[9], 1), 0, 1)
    return {"amplitudes": amplitudes, "exchange_ints": exchange_ints, "virt_fock": virt_fock, "intersection": intersection, "occ_fock": occ_fock, "virt_energy": virt_energy, "fock_tiles": fock_tiles, "intersection_tiles": intersection_tiles, "occ_pattern": occ_pattern, "pair_domain": pair_domain}


HIGHEST = lax.Precision.HIGHEST


def expand_tiles(tiles):
    return jnp.repeat(jnp.repeat(tiles.astype(jnp.float32), TILE, axis=0), TILE, axis=1)


def sandwich(left_mat, blocks, right_mat):
    partial_value = jnp.einsum('jab,bc->jac', blocks, right_mat, precision=HIGHEST)
    return jnp.einsum('ac,jcb->jab', left_mat, partial_value, precision=HIGHEST)


def reference(amplitudes, exchange_ints, virt_fock, intersection, occ_fock, virt_energy, fock_tiles, intersection_tiles, occ_pattern, pair_domain):
    fock_eff = virt_fock * expand_tiles(fock_tiles)
    over_eff = intersection * expand_tiles(intersection_tiles)
    coupling = occ_fock * occ_pattern.astype(jnp.float32)
    occ_diag = jnp.diagonal(occ_fock)
    domain = jnp.repeat(pair_domain.astype(jnp.float32), TILE, axis=2)
    current = amplitudes
    for iteration in range(ITERS):
        def row_half(pieces):
            blocks, couple_row = pieces
            coupled = jnp.einsum('k,kjab->jab', couple_row, current, precision=HIGHEST)
            return sandwich(fock_eff, blocks, over_eff) - sandwich(over_eff, coupled, over_eff)

        half_resid = lax.map(row_half, (current, coupling))
        mirrored = jnp.transpose(half_resid, (1, 0, 3, 2))
        residual = exchange_ints + half_resid + mirrored

        def row_update(pieces):
            blocks, resid_row, domain_row, occ_value = pieces
            denominator = virt_energy[None, :, None] + virt_energy[None, None, :] - occ_value - occ_diag[:, None, None]
            step_scale = domain_row[:, :, None] * domain_row[:, None, :] / denominator
            return blocks - step_scale * resid_row

        current = lax.map(row_update, (current, residual, domain, occ_diag))
    return current
```

```python
import functools
import math
import random

import jax
import jax.numpy as jnp
import numpy as np
from jax import lax
from jax.experimental import pallas as pl
from jax.experimental.pallas import tpu as pltpu
from jax.sharding import PartitionSpec as P

ITERS = 2
AXES = ("row", "col")
PAD = 8


def slot_of(i, j):
    if i == j:
        return i % 2
    return (i + j + (i > j)) % 2


def list_units(count):
    units = [((i, j), (j, i)) for i in range(count) for j in range(i + 1, count)]
    units += [((i, i), (i + 1, i + 1)) for i in range(0, count, 2)]
    return [tuple(sorted(unit, key=lambda block: slot_of(*block))) for unit in units]


def first_hosts(units, cols):
    hosts = []
    for unit in units:
        i, j = min(unit[0], unit[1])
        if unit[0][0] == unit[0][1]:
            hosts.append((i + 1) * cols + i // 2)
        elif i // 2 == j // 2:
            hosts.append(i * cols + j // 2)
        elif (i + j) % 2 == 0:
            hosts.append(i * cols + j // 2)
        else:
            hosts.append(j * cols + i // 2)
    return hosts


def chip_coords(mesh, cols):
    devices = list(mesh.devices.flat)
    if all(getattr(d, "coords", None) is not None for d in devices):
        return [tuple(d.coords) for d in devices]
    return [(k % cols // 2, k // cols, 0) for k in range(len(devices))]


def route_matrix(chips):
    index = {chip: k for k, chip in enumerate(chips)}
    links = {}
    rows = []
    for a in chips:
        for b in chips:
            here, path = list(a), []
            for axis in (2, 0, 1):
                while here[axis] != b[axis]:
                    there = list(here)
                    there[axis] += 1 if b[axis] > here[axis] else -1
                    if tuple(there) not in index:
                        return None
                    path.append(links.setdefault((tuple(here), tuple(there)), len(links)))
                    here = there
            rows.append(path)
    matrix = np.zeros((len(rows), max(1, len(links))), np.float32)
    for k, path in enumerate(rows):
        matrix[k, path] = 1.0
    return matrix


def choose_hosts(mesh, units, count, cols):
    hosts = first_hosts(units, cols)
    coords = chip_coords(mesh, cols)
    chips = sorted(set(coords))
    if len(chips) > 32:
        return hosts
    routes = route_matrix(chips)
    if routes is None:
        return hosts
    number = len(chips)
    chip_of_device = np.array([chips.index(c) for c in coords])
    block_unit = np.zeros((count, count), np.int64)
    for u, unit in enumerate(units):
        for i, j in unit:
            block_unit[i, j] = u
    owner = np.array([[chip_of_device[i * cols + j // 2] for j in range(count)] for i in range(count)])
    up = np.concatenate([block_unit[:-1].ravel(), block_unit[1:].ravel()])
    down = np.concatenate([block_unit[1:].ravel(), block_unit[:-1].ravel()])
    flat_unit, flat_owner = block_unit.ravel(), owner.ravel()
    pairs = number * number

    def price(hosts):
        at = chip_of_device[hosts]
        here = at[flat_unit]
        keys = np.concatenate(
            [flat_owner * number + here, pairs + here * number + flat_owner, 2 * pairs + at[up] * number + at[down]]
        )
        there, back, halo = np.bincount(keys, minlength=3 * pairs).reshape(3, pairs).astype(np.float32) @ routes
        peak = there.max() + back.max() + halo.max() + (halo + there).max()
        return float(peak + 0.001 * (there @ there + back @ back + halo @ halo))

    draw = random.Random(7)
    best_cost, best = math.inf, None
    total = 16000
    for attempt in range(3):
        current = np.array(hosts)
        cost = price(current)
        for step in range(total):
            heat = 2.0 * 0.02 ** (step / total)
            a, b = draw.randrange(len(units)), draw.randrange(len(units))
            current[[a, b]] = current[[b, a]]
            trial = price(current)
            if trial <= cost or math.exp((cost - trial) / heat) > draw.random():
                cost = trial
                if cost < best_cost:
                    best_cost, best = cost, current.copy()
            else:
                current[[a, b]] = current[[b, a]]
    return [int(h) for h in best]


def two_colours(edges):
    by_end = {}
    for k, (source, target) in enumerate(edges):
        by_end.setdefault(("s", source), []).append(k)
        by_end.setdefault(("t", target), []).append(k)
    colour = {}
    for start in range(len(edges)):
        stack = [] if start in colour else [start]
        if stack:
            colour[start] = 0
        while stack:
            k = stack.pop()
            for end in (("s", edges[k][0]), ("t", edges[k][1])):
                for other in by_end[end]:
                    if other not in colour:
                        colour[other] = 1 - colour[k]
                        stack.append(other)
    assert all(len({colour[k] for k in ks}) == len(ks) for ks in by_end.values())
    return [colour[k] for k in range(len(edges))]


def make_plan(mesh, count):
    rows, cols = mesh.shape["row"], mesh.shape["col"]
    assert count == rows and count == 2 * cols
    units = list_units(count)
    hosts = choose_hosts(mesh, units, count, cols)
    host = {}
    for unit, device in zip(units, hosts):
        for block in unit:
            host[block] = device
    devices = rows * cols
    table = np.zeros((devices, 16), np.int32)
    first = np.zeros((devices,), np.int32)
    gather = [[], []]
    for unit, device in zip(units, hosts):
        for s, (i, j) in enumerate(unit):
            owner = i * cols + j // 2
            gather[s].append((owner, device))
            if s == 0:
                first[owner] = j % 2
            table[device, 2 * s : 2 * s + 2] = (i, j)
        table[device, 4] = int(unit[0][0] == unit[0][1])
    table[:, 9:13] = -1
    halo = []
    for s in range(2):
        moves = [
            (i, j, k)
            for i in range(count)
            for j in range(count)
            if slot_of(i, j) == s
            for k in (i - 1, i + 1)
            if 0 <= k < count
        ]
        edges = [(host[i, j], host[k, j]) for i, j, k in moves]
        colours = two_colours(edges)
        for colour in range(2):
            number = len(halo)
            halo.append([e for e, c in zip(edges, colours) if c == colour])
            for (i, j, k), (_, target), c in zip(moves, edges, colours):
                if c == colour:
                    table[target, 5 + number] = i
                    table[target, 9 + number] = slot_of(k, j)
    return table, first, gather, halo


DOT = functools.partial(lax.dot_general, preferred_element_type=jnp.float32)
MATMUL = (((1,), (0,)), ((), ()))


def split(value):
    high = value.astype(jnp.bfloat16)
    low = (value - high.astype(jnp.float32)).astype(jnp.bfloat16)
    return high, low


def constants_kernel(fock_tiles, over_tiles, fock, over, fock_left, over_left, over_right):
    size = fock.shape[0]
    tiles = fock_tiles.shape[0]
    tile = size // tiles
    for a in range(tiles):
        for b in range(tiles):
            rows, cols = pl.ds(a * tile, tile), pl.ds(b * tile, tile)
            high, low = split(fock[rows, cols] * fock_tiles[a, b].astype(jnp.float32))
            for part, value in enumerate((high, high, low)):
                fock_left[rows, pl.ds(part * size + b * tile, tile)] = value
            high, low = split(over[rows, cols] * over_tiles[a, b].astype(jnp.float32))
            for part, value in enumerate((high, high, low)):
                over_left[rows, pl.ds(part * size + b * tile, tile)] = value
            for part, value in enumerate((high, low, high)):
                over_right[pl.ds(part * size + a * tile, tile), cols] = value


def stack_right(parts, stack):
    size = parts[0].shape[0]
    for s, value in enumerate(parts):
        high, low = split(value)
        for part, piece in enumerate((high, low, high)):
            stack[pl.ds(part * size, size), pl.ds(s * size, size)] = piece


def own_kernel(x0, x1, fock_left, out, stack):
    stack_right((x0[...], x1[...]), stack)
    out[...] = DOT(fock_left[...], stack[...], MATMUL)


def update_kernel(
    table, occ, pattern, own, x0, x1, r0, r1, r2, r3, k0, k1, over_left, over_right, e_col, e_row, y0, y1, stack, left
):
    size = x0.shape[0]
    halo = (r0, r1, r2, r3)

    def couple(i, k):
        return occ[i, k] * pattern[i, k].astype(jnp.float32)

    coupled = []
    for s, x in enumerate((x0, x1)):
        i = table[2 * s]
        value = couple(i, i) * x[...]
        for k, r in enumerate(halo):
            value += jnp.where(table[9 + k] == s, couple(i, table[5 + k]), 0.0) * r[...]
        coupled.append(value)
    stack_right(coupled, stack)
    half = own[...] - DOT(over_left[...], stack[...], MATMUL)
    for s in range(2):
        high, low = split(half[:, s * size : (s + 1) * size])
        for part, piece in enumerate((high, high, low)):
            left[pl.ds(s * size, size), pl.ds(part * size, size)] = piece
    half = DOT(left[...], over_right[...], MATMUL)
    g0, g1 = half[:size], half[size:]
    alone = table[4] == 1
    mirrored = (jnp.where(alone, g0, g1).T, jnp.where(alone, g1, g0).T)
    for s, (x, k, g, y) in enumerate(((x0, k0, g0, y0), (x1, k1, g1, y1))):
        i, j = table[2 * s], table[2 * s + 1]
        mask = k[pl.ds(size, PAD), :]
        mask = DOT(mask, mask, (((0,), (0,)), ((), ())))
        scale = mask / (e_col[...] + e_row[...] - occ[i, i] - occ[j, j])
        y[...] = x[...] - scale * (k[pl.ds(0, size), :] + g + mirrored[s])


SMEM = functools.partial(pl.BlockSpec, memory_space=pltpu.SMEM)
VMEM = functools.partial(pl.BlockSpec, memory_space=pltpu.VMEM)


def constants(fock_tiles, over_tiles, fock, over):
    size = fock.shape[0]
    wide = jax.ShapeDtypeStruct((size, 3 * size), jnp.bfloat16)
    return pl.pallas_call(
        constants_kernel,
        in_specs=[SMEM(), SMEM(), VMEM(), VMEM()],
        out_specs=[VMEM()] * 3,
        out_shape=[wide, wide, jax.ShapeDtypeStruct((3 * size, size), jnp.bfloat16)],
    )(fock_tiles, over_tiles, fock, over)


def own_part(x0, x1, fock_left):
    size = x0.shape[0]
    return pl.pallas_call(
        own_kernel,
        in_specs=[VMEM()] * 3,
        out_specs=VMEM(),
        out_shape=jax.ShapeDtypeStruct((size, 2 * size), jnp.float32),
        scratch_shapes=[pltpu.VMEM((3 * size, 2 * size), jnp.bfloat16)],
    )(x0, x1, fock_left)


def update(table, occ, pattern, own, x, halo, k, over_left, over_right, e_col, e_row):
    size = x[0].shape[0]
    block = jax.ShapeDtypeStruct((size, size), jnp.float32)
    return pl.pallas_call(
        update_kernel,
        in_specs=[SMEM()] * 3 + [VMEM()] * 13,
        out_specs=[VMEM()] * 2,
        out_shape=[block, block],
        scratch_shapes=[
            pltpu.VMEM((3 * size, 2 * size), jnp.bfloat16),
            pltpu.VMEM((2 * size, 3 * size), jnp.bfloat16),
        ],
    )(table, occ, pattern, own, *x, *halo, *k, over_left, over_right, e_col, e_row)


def solution(mesh):
    def shards(amplitudes, exchange_ints, fock, over, occ, energy, fock_tiles, over_tiles, pattern, domain):
        count, size = occ.shape[0], fock.shape[0]
        assert amplitudes.shape[:2] == (1, 2)
        table, first, gather, halo = make_plan(mesh, count)
        device = lax.axis_index("row") * mesh.shape["col"] + lax.axis_index("col")
        table = lax.dynamic_index_in_dim(jnp.asarray(table), device, keepdims=False)
        first = lax.dynamic_index_in_dim(jnp.asarray(first), device, keepdims=False)
        picks = (first, 1 - first)

        x = [
            lax.ppermute(lax.dynamic_index_in_dim(amplitudes[0], p, keepdims=False), AXES, moves)
            for p, moves in zip(picks, gather)
        ]
        tile = size // fock_tiles.shape[0]
        masks = jnp.repeat(domain[0].astype(jnp.float32), tile, axis=1)
        masks = jnp.pad(masks[:, None, :], ((0, 0), (0, PAD - 1), (0, 0)))
        payload = jnp.concatenate([exchange_ints[0], masks], axis=1)
        payload = [lax.dynamic_index_in_dim(payload, p, keepdims=False) for p in picks]
        payload, x = lax.optimization_barrier((payload, x))
        fock_left, over_left, over_right = constants(fock_tiles, over_tiles, fock, over)
        e_col, e_row = energy[:, None], energy[None, :]
        k = None
        for _ in range(ITERS):
            nearby = [lax.ppermute(x[n // 2], AXES, moves) for n, moves in enumerate(halo)]
            if k is None:
                k = [lax.ppermute(p, AXES, moves) for p, moves in zip(payload, gather)]
            own = own_part(*x, fock_left)
            x = update(table, occ, pattern, own, x, nearby, k, over_left, over_right, e_col, e_row)
        back = [
            lax.ppermute(value, AXES, [(target, source) for source, target in moves])
            for value, moves in zip(x, gather)
        ]
        out = jnp.where(first == 0, jnp.stack(back), jnp.stack(back[::-1]))
        return out[None]

    blocks = P("row", "col", None, None)
    in_specs = (blocks, blocks, P(), P(), P(), P(), P(), P(), P(), P("row", "col", None))
    return jax.shard_map(shards, mesh=mesh, in_specs=in_specs, out_specs=blocks, check_vma=False)
```

```python
import functools

import jax
import jax.numpy as jnp
import numpy as np
from jax import lax
from jax.experimental import pallas as pl
from jax.experimental.pallas import tpu as pltpu
from jax.sharding import PartitionSpec as P

ITERS = 2
AXES = ("row", "col")
PAD = 8


def slot_of(i, j):
    if i == j:
        return i % 2
    return (i + j + (i > j)) % 2


def list_units(count):
    units = [((i, j), (j, i)) for i in range(count) for j in range(i + 1, count)]
    units += [((i, i), (i + 1, i + 1)) for i in range(0, count, 2)]
    return [tuple(sorted(unit, key=lambda block: slot_of(*block))) for unit in units]


def first_hosts(units, cols):
    hosts = []
    for unit in units:
        i, j = min(unit[0], unit[1])
        if unit[0][0] == unit[0][1]:
            hosts.append((i + 1) * cols + i // 2)
        elif i // 2 == j // 2:
            hosts.append(i * cols + j // 2)
        elif (i + j) % 2 == 0:
            hosts.append(i * cols + j // 2)
        else:
            hosts.append(j * cols + i // 2)
    return hosts


def chip_coords(mesh, cols):
    devices = list(mesh.devices.flat)
    if all(getattr(d, "coords", None) is not None for d in devices):
        return [tuple(d.coords) for d in devices]
    return [(k % cols // 2, k // cols, 0) for k in range(len(devices))]


def route_matrix(chips):
    index = {chip: k for k, chip in enumerate(chips)}
    links = {}
    rows = []
    for a in chips:
        for b in chips:
            here, path = list(a), []
            for axis in (2, 0, 1):
                while here[axis] != b[axis]:
                    there = list(here)
                    there[axis] += 1 if b[axis] > here[axis] else -1
                    if tuple(there) not in index:
                        return None
                    path.append(links.setdefault((tuple(here), tuple(there)), len(links)))
                    here = there
            rows.append(path)
    matrix = np.zeros((len(rows), max(1, len(links))), np.float32)
    for k, path in enumerate(rows):
        matrix[k, path] = 1.0
    return matrix


def choose_hosts(mesh, units, count, cols):
    hosts = first_hosts(units, cols)
    coords = chip_coords(mesh, cols)
    chips = sorted(set(coords))
    if len(chips) > 32:
        return hosts
    routes = route_matrix(chips)
    if routes is None:
        return hosts
    number = len(chips)
    chip_of_device = np.array([chips.index(c) for c in coords])
    block_unit = np.zeros((count, count), np.int64)
    for u, unit in enumerate(units):
        for i, j in unit:
            block_unit[i, j] = u
    owner = np.array([[chip_of_device[i * cols + j // 2] for j in range(count)] for i in range(count)])
    up = np.concatenate([block_unit[:-1].ravel(), block_unit[1:].ravel()])
    down = np.concatenate([block_unit[1:].ravel(), block_unit[:-1].ravel()])
    flat_unit, flat_owner = block_unit.ravel(), owner.ravel()
    pairs = number * number

    chains, steps = 24, 12000
    draw = np.random.RandomState(7)
    offset = (np.arange(chains) * 3 * pairs)[:, None]

    def price(hosts):
        at = chip_of_device[hosts]
        here = at[:, flat_unit]
        keys = [flat_owner * number + here, pairs + here * number + flat_owner, 2 * pairs + at[:, up] * number + at[:, down]]
        keys = np.concatenate(keys, axis=1) + offset
        flows = np.bincount(keys.ravel(), minlength=3 * pairs * chains).astype(np.float32)
        loads = (flows.reshape(-1, pairs) @ routes).reshape(chains, 3, -1)
        there, back, halo = loads[:, 0], loads[:, 1], loads[:, 2]
        peak = there.max(1) + back.max(1) + halo.max(1) + (halo + there).max(1)
        return peak + 0.01 * (loads * loads).sum((1, 2))

    current = np.tile(np.array(hosts), (chains, 1))
    cost = price(current)
    best_cost, best = cost.min(), current[cost.argmin()].copy()
    each = np.arange(chains)
    for step in range(steps):
        heat = 1.5 * 0.02 ** (step / steps)
        a, b = draw.randint(len(units), size=(2, chains))
        trial = current.copy()
        trial[each, a], trial[each, b] = current[each, b], current[each, a]
        trial_cost = price(trial)
        take = (trial_cost <= cost) | (np.exp(np.minimum(0.0, (cost - trial_cost) / heat)) > draw.random_sample(chains))
        current[take], cost[take] = trial[take], trial_cost[take]
        if cost.min() < best_cost:
            best_cost, best = cost.min(), current[cost.argmin()].copy()
    return [int(h) for h in best]


def two_colours(edges):
    by_end = {}
    for k, (source, target) in enumerate(edges):
        by_end.setdefault(("s", source), []).append(k)
        by_end.setdefault(("t", target), []).append(k)
    colour = {}
    for start in range(len(edges)):
        stack = [] if start in colour else [start]
        if stack:
            colour[start] = 0
        while stack:
            k = stack.pop()
            for end in (("s", edges[k][0]), ("t", edges[k][1])):
                for other in by_end[end]:
                    if other not in colour:
                        colour[other] = 1 - colour[k]
                        stack.append(other)
    assert all(len({colour[k] for k in ks}) == len(ks) for ks in by_end.values())
    return [colour[k] for k in range(len(edges))]


def make_plan(mesh, count):
    rows, cols = mesh.shape["row"], mesh.shape["col"]
    assert count == rows and count == 2 * cols
    units = list_units(count)
    hosts = choose_hosts(mesh, units, count, cols)
    host = {}
    for unit, device in zip(units, hosts):
        for block in unit:
            host[block] = device
    devices = rows * cols
    table = np.zeros((devices, 16), np.int32)
    gather = [[], []]
    for unit, device in zip(units, hosts):
        for s, (i, j) in enumerate(unit):
            owner = i * cols + j // 2
            gather[s].append((owner, device))
            table[device, 2 * s : 2 * s + 2] = (i, j)
        table[device, 4] = int(unit[0][0] == unit[0][1])
    table[:, 9:13] = -1
    halo = []
    for s in range(2):
        moves = [
            (i, j, k)
            for i in range(count)
            for j in range(count)
            if slot_of(i, j) == s
            for k in (i - 1, i + 1)
            if 0 <= k < count
        ]
        edges = [(host[i, j], host[k, j]) for i, j, k in moves]
        colours = two_colours(edges)
        for colour in range(2):
            number = len(halo)
            halo.append([e for e, c in zip(edges, colours) if c == colour])
            for (i, j, k), (_, target), c in zip(moves, edges, colours):
                if c == colour:
                    table[target, 5 + number] = i
                    table[target, 9 + number] = slot_of(k, j)
    return table, gather, halo


DOT = functools.partial(lax.dot_general, preferred_element_type=jnp.float32)
MATMUL = (((1,), (0,)), ((), ()))


def split(value):
    high = value.astype(jnp.bfloat16)
    low = (value - high.astype(jnp.float32)).astype(jnp.bfloat16)
    return high, low


def constants_kernel(fock_tiles, over_tiles, fock, over, fock_left, over_left, over_right):
    size = fock.shape[0]
    tiles = fock_tiles.shape[0]
    tile = size // tiles
    for a in range(tiles):
        for b in range(tiles):
            rows, cols = pl.ds(a * tile, tile), pl.ds(b * tile, tile)
            high, low = split(fock[rows, cols] * fock_tiles[a, b].astype(jnp.float32))
            for part, value in enumerate((high, high, low)):
                fock_left[rows, pl.ds(part * size + b * tile, tile)] = value
            high, low = split(over[rows, cols] * over_tiles[a, b].astype(jnp.float32))
            for part, value in enumerate((high, high, low)):
                over_left[rows, pl.ds(part * size + b * tile, tile)] = value
            for part, value in enumerate((high, low, high)):
                over_right[pl.ds(part * size + a * tile, tile), cols] = value


def stack_right(parts, stack):
    size = parts[0].shape[0]
    for s, value in enumerate(parts):
        high, low = split(value)
        for part, piece in enumerate((high, low, high)):
            stack[pl.ds(part * size, size), pl.ds(s * size, size)] = piece


def first_slot():
    i, j = lax.axis_index("row"), lax.axis_index("col") * 2
    return (i + (i > j).astype(jnp.int32)) % 2


def pick_kernel(blocks, out0, out1, near, sems):
    first = first_slot()
    slots, outs = (first, 1 - first), (out0, out1)
    into = [pltpu.make_async_copy(blocks.at[slots[s]], near.at[s], sems.at[s]) for s in range(2)]
    back = [pltpu.make_async_copy(near.at[s], outs[s], sems.at[2 + s]) for s in range(2)]
    for copy in into:
        copy.start()
    for s in range(2):
        into[s].wait()
        back[s].start()
    for copy in back:
        copy.wait()


def pick_masked_kernel(domain, blocks, out0, out1, near, sems):
    size = blocks.shape[1]
    tiles = domain.shape[1]
    tile = size // tiles
    first = first_slot()
    slots, outs = (first, 1 - first), (out0, out1)
    body = pl.ds(0, size)
    into = [pltpu.make_async_copy(blocks.at[slots[s]], near.at[s, body], sems.at[s]) for s in range(2)]
    back = [pltpu.make_async_copy(near.at[s], outs[s], sems.at[2 + s]) for s in range(2)]
    for copy in into:
        copy.start()
    top = lax.broadcasted_iota(jnp.int32, (PAD, tile), 0) == 0
    for s in range(2):
        for t in range(tiles):
            value = domain[slots[s], t].astype(jnp.float32)
            near[s, pl.ds(size, PAD), pl.ds(t * tile, tile)] = jnp.where(top, value, 0.0)
    for s in range(2):
        into[s].wait()
        back[s].start()
    for copy in back:
        copy.wait()


def place_kernel(in0, in1, out, sems):
    first = first_slot()
    copies = [
        pltpu.make_async_copy(in0, out.at[first], sems.at[0]),
        pltpu.make_async_copy(in1, out.at[1 - first], sems.at[1]),
    ]
    for copy in copies:
        copy.start()
    for copy in copies:
        copy.wait()


def own_kernel(x0, x1, fock_left, out, stack):
    stack_right((x0[...], x1[...]), stack)
    out[...] = DOT(fock_left[...], stack[...], MATMUL)


def scale_kernel(table, occ, x0, x1, k0, k1, e_col, e_row, scale, start):
    size = x0.shape[0]
    for s, (x, k) in enumerate(((x0, k0), (x1, k1))):
        i, j = table[2 * s], table[2 * s + 1]
        mask = k[pl.ds(size, PAD), :]
        mask = DOT(mask, mask, (((0,), (0,)), ((), ())))
        value = mask / (e_col[...] + e_row[...] - occ[i, i] - occ[j, j])
        scale[s] = value
        start[s] = x[...] - value * k[pl.ds(0, size), :]


def update_kernel(
    table, occ, pattern, x0, x1, r0, r1, r2, r3, own, over_left, over_right, scale, start,
    y0, y1, near, own_v, left_v, right_v, scale_v, start_v, stack, left, g, near_sems, sems,
):
    size = x0.shape[0]
    chunks = near_sems.shape[0]
    rows = size // chunks
    blocks = (x0, x1, r0, r1, r2, r3)

    def near_copy(n, b):
        part = pl.ds(n * rows, rows)
        return pltpu.make_async_copy(blocks[b].at[part], near.at[b, part], near_sems.at[n, b])

    others = [
        pltpu.make_async_copy(source, target, sems.at[n])
        for n, (source, target) in enumerate(
            ((over_left, left_v), (own, own_v), (over_right, right_v), (scale, scale_v), (start, start_v))
        )
    ]
    for n in range(chunks):
        for b in range(len(blocks)):
            near_copy(n, b).start()
    for copy in others:
        copy.start()

    def couple(i, k):
        return occ[i, k] * pattern[i, k].astype(jnp.float32)

    own_c, halo_c = [], []
    for s in range(2):
        i = table[2 * s]
        own_c.append(couple(i, i))
        halo_c.append([jnp.where(table[9 + k] == s, couple(i, table[5 + k]), 0.0) for k in range(4)])
    for n in range(chunks):
        part = pl.ds(n * rows, rows)
        for b in range(len(blocks)):
            near_copy(n, b).wait()
        for s in range(2):
            value = own_c[s] * near[s, part, :]
            for k in range(4):
                value += halo_c[s][k] * near[2 + k, part, :]
            high, low = split(value)
            for q, piece in enumerate((high, low, high)):
                stack[pl.ds(q * size + n * rows, rows), pl.ds(s * size, size)] = piece
    others[0].wait()
    others[1].wait()
    half = own_v[...] - DOT(left_v[...], stack[...], MATMUL)
    for s in range(2):
        high, low = split(half[:, s * size : (s + 1) * size])
        for q, piece in enumerate((high, high, low)):
            left[pl.ds(s * size, size), pl.ds(q * size, size)] = piece
    others[2].wait()
    half = DOT(left[...], right_v[...], MATMUL)
    g[0], g[1] = half[:size], half[size:]
    others[3].wait()
    others[4].wait()
    other = 1 - table[4]
    for s, y in enumerate((y0, y1)):
        mirror = g[other if s == 0 else 1 - other]
        y[...] = start_v[s] - scale_v[s] * (g[s] + mirror.T)


SMEM = functools.partial(pl.BlockSpec, memory_space=pltpu.SMEM)
VMEM = functools.partial(pl.BlockSpec, memory_space=pltpu.VMEM)
ANY = functools.partial(pl.BlockSpec, memory_space=pl.ANY)


def constants(fock_tiles, over_tiles, fock, over):
    size = fock.shape[0]
    wide = jax.ShapeDtypeStruct((size, 3 * size), jnp.bfloat16)
    return pl.pallas_call(
        constants_kernel,
        in_specs=[SMEM(), SMEM(), VMEM(), VMEM()],
        out_specs=[VMEM()] * 3,
        out_shape=[wide, wide, jax.ShapeDtypeStruct((3 * size, size), jnp.bfloat16)],
    )(fock_tiles, over_tiles, fock, over)


def pick(blocks):
    block = jax.ShapeDtypeStruct(blocks.shape[1:], blocks.dtype)
    return pl.pallas_call(
        pick_kernel,
        in_specs=[ANY()],
        out_specs=[ANY()] * 2,
        out_shape=[block] * 2,
        scratch_shapes=[pltpu.VMEM(blocks.shape, blocks.dtype), pltpu.SemaphoreType.DMA((4,))],
    )(blocks)


def pick_masked(blocks, domain):
    size = blocks.shape[1]
    block = jax.ShapeDtypeStruct((size + PAD, size), blocks.dtype)
    return pl.pallas_call(
        pick_masked_kernel,
        in_specs=[SMEM(), ANY()],
        out_specs=[ANY()] * 2,
        out_shape=[block] * 2,
        scratch_shapes=[pltpu.VMEM((2, size + PAD, size), jnp.float32), pltpu.SemaphoreType.DMA((4,))],
    )(domain, blocks)


def place(pieces):
    return pl.pallas_call(
        place_kernel,
        in_specs=[VMEM()] * 2,
        out_specs=ANY(),
        out_shape=jax.ShapeDtypeStruct((2, *pieces[0].shape), pieces[0].dtype),
        scratch_shapes=[pltpu.SemaphoreType.DMA((2,))],
    )(*pieces)


def own_part(x, fock_left):
    size = x[0].shape[0]
    return pl.pallas_call(
        own_kernel,
        in_specs=[VMEM()] * 3,
        out_specs=VMEM(),
        out_shape=jax.ShapeDtypeStruct((size, 2 * size), jnp.float32),
        scratch_shapes=[pltpu.VMEM((3 * size, 2 * size), jnp.bfloat16)],
    )(*x, fock_left)


def scale_part(table, occ, x, k, e_col, e_row):
    size = x[0].shape[0]
    pair = jax.ShapeDtypeStruct((2, size, size), jnp.float32)
    return pl.pallas_call(
        scale_kernel,
        in_specs=[SMEM()] * 2 + [VMEM()] * 6,
        out_specs=[VMEM()] * 2,
        out_shape=[pair, pair],
    )(table, occ, *x, *k, e_col, e_row)


def update(table, occ, pattern, x, halo, own, over_left, over_right, scale, start):
    size = x[0].shape[0]
    block = jax.ShapeDtypeStruct((size, size), jnp.float32)
    chunks = 3
    pair = pltpu.VMEM((2, size, size), jnp.float32)
    return pl.pallas_call(
        update_kernel,
        in_specs=[SMEM()] * 3 + [ANY()] * 11,
        out_specs=[VMEM()] * 2,
        out_shape=[block, block],
        scratch_shapes=[
            pltpu.VMEM((6, size, size), jnp.float32),
            pltpu.VMEM(own.shape, jnp.float32),
            pltpu.VMEM(over_left.shape, jnp.bfloat16),
            pltpu.VMEM(over_right.shape, jnp.bfloat16),
            pair,
            pair,
            pltpu.VMEM((3 * size, 2 * size), jnp.bfloat16),
            pltpu.VMEM((2 * size, 3 * size), jnp.bfloat16),
            pair,
            pltpu.SemaphoreType.DMA((chunks, 6)),
            pltpu.SemaphoreType.DMA((5,)),
        ],
    )(table, occ, pattern, *x, *halo, own, over_left, over_right, scale, start)


def solution(mesh):
    def shards(amplitudes, exchange_ints, fock, over, occ, energy, fock_tiles, over_tiles, pattern, domain):
        count = occ.shape[0]
        assert amplitudes.shape[:2] == (1, 2)
        table, gather, halo = make_plan(mesh, count)
        device = lax.axis_index("row") * mesh.shape["col"] + lax.axis_index("col")
        table = lax.dynamic_index_in_dim(jnp.asarray(table), device, keepdims=False)
        own_x = pick(amplitudes[0])
        x = [lax.ppermute(value, AXES, moves) for value, moves in zip(own_x, gather)]
        integrals, own_x = lax.optimization_barrier((exchange_ints, own_x))
        own_k = pick_masked(integrals[0], domain[0])
        k = [lax.ppermute(value, AXES, moves) for value, moves in zip(own_k, gather)]
        fock_left, over_left, over_right = constants(fock_tiles, over_tiles, fock, over)
        e_col, e_row = energy[:, None], energy[None, :]
        for _ in range(ITERS):
            nearby = [lax.ppermute(x[n // 2], AXES, moves) for n, moves in enumerate(halo)]
            own = own_part(x, fock_left)
            scale, start = scale_part(table, occ, x, k, e_col, e_row)
            x = update(table, occ, pattern, x, nearby, own, over_left, over_right, scale, start)
        back = [
            lax.ppermute(value, AXES, [(target, source) for source, target in moves])
            for value, moves in zip(x, gather)
        ]
        return place(back)[None]

    blocks = P("row", "col", None, None)
    in_specs = (blocks, blocks, P(), P(), P(), P(), P(), P(), P(), P("row", "col", None))
    return jax.shard_map(shards, mesh=mesh, in_specs=in_specs, out_specs=blocks, check_vma=False)
```

```python
import functools

import jax
import jax.numpy as jnp
import numpy as np
from jax import lax
from jax.experimental import pallas as pl
from jax.experimental.pallas import tpu as pltpu
from jax.sharding import PartitionSpec as P

ITERS = 2
AXES = ("row", "col")
PAD = 8


def slot_of(i, j):
    if i == j:
        return i % 2
    return (i + j + (i > j)) % 2


def list_units(count):
    units = [((i, j), (j, i)) for i in range(count) for j in range(i + 1, count)]
    units += [((i, i), (i + 1, i + 1)) for i in range(0, count, 2)]
    return [tuple(sorted(unit, key=lambda block: slot_of(*block))) for unit in units]


def first_hosts(units, cols):
    hosts = []
    for unit in units:
        i, j = min(unit[0], unit[1])
        if unit[0][0] == unit[0][1]:
            hosts.append((i + 1) * cols + i // 2)
        elif i // 2 == j // 2:
            hosts.append(i * cols + j // 2)
        elif (i + j) % 2 == 0:
            hosts.append(i * cols + j // 2)
        else:
            hosts.append(j * cols + i // 2)
    return hosts


def chip_coords(mesh, cols):
    devices = list(mesh.devices.flat)
    if all(getattr(d, "coords", None) is not None for d in devices):
        return [tuple(d.coords) for d in devices]
    return [(k % cols // 2, k // cols, 0) for k in range(len(devices))]


def route_matrix(chips):
    index = {chip: k for k, chip in enumerate(chips)}
    links = {}
    rows = []
    for a in chips:
        for b in chips:
            here, path = list(a), []
            for axis in (2, 0, 1):
                while here[axis] != b[axis]:
                    there = list(here)
                    there[axis] += 1 if b[axis] > here[axis] else -1
                    if tuple(there) not in index:
                        return None
                    path.append(links.setdefault((tuple(here), tuple(there)), len(links)))
                    here = there
            rows.append(path)
    matrix = np.zeros((len(rows), max(1, len(links))), np.float32)
    for k, path in enumerate(rows):
        matrix[k, path] = 1.0
    return matrix


def choose_hosts(mesh, units, count, cols):
    hosts = first_hosts(units, cols)
    coords = chip_coords(mesh, cols)
    chips = sorted(set(coords))
    if len(chips) > 32:
        return hosts
    routes = route_matrix(chips)
    if routes is None:
        return hosts
    number = len(chips)
    chip_of_device = np.array([chips.index(c) for c in coords])
    block_unit = np.zeros((count, count), np.int64)
    for u, unit in enumerate(units):
        for i, j in unit:
            block_unit[i, j] = u
    owner = np.array([[chip_of_device[i * cols + j // 2] for j in range(count)] for i in range(count)])
    up = np.concatenate([block_unit[:-1].ravel(), block_unit[1:].ravel()])
    down = np.concatenate([block_unit[1:].ravel(), block_unit[:-1].ravel()])
    flat_unit, flat_owner = block_unit.ravel(), owner.ravel()
    pairs = number * number

    chains, steps = 32, 10000
    draw = np.random.RandomState(78)
    offset = (np.arange(chains) * 3 * pairs)[:, None]

    def price(hosts):
        at = chip_of_device[hosts]
        here = at[:, flat_unit]
        keys = [flat_owner * number + here, pairs + here * number + flat_owner, 2 * pairs + at[:, up] * number + at[:, down]]
        keys = np.concatenate(keys, axis=1) + offset
        flows = np.bincount(keys.ravel(), minlength=3 * pairs * chains).astype(np.float32)
        loads = (flows.reshape(-1, pairs) @ routes).reshape(chains, 3, -1)
        there, back, halo = loads[:, 0], loads[:, 1], loads[:, 2]
        peak = there.max(1) + back.max(1) + 2.0 * halo.max(1) + 0.3 * (halo + 2.0 * there).max(1)
        return peak + 0.01 * (loads * loads).sum((1, 2))

    current = np.tile(np.array(hosts), (chains, 1))
    cost = price(current)
    best_cost, best = cost.min(), current[cost.argmin()].copy()
    each = np.arange(chains)
    for step in range(steps):
        heat = 1.5 * 0.02 ** (step / steps)
        a, b = draw.randint(len(units), size=(2, chains))
        trial = current.copy()
        trial[each, a], trial[each, b] = current[each, b], current[each, a]
        trial_cost = price(trial)
        take = (trial_cost <= cost) | (np.exp(np.minimum(0.0, (cost - trial_cost) / heat)) > draw.random_sample(chains))
        current[take], cost[take] = trial[take], trial_cost[take]
        if cost.min() < best_cost:
            best_cost, best = cost.min(), current[cost.argmin()].copy()
    return [int(h) for h in best]


def two_colours(edges):
    by_end = {}
    for k, (source, target) in enumerate(edges):
        by_end.setdefault(("s", source), []).append(k)
        by_end.setdefault(("t", target), []).append(k)
    colour = {}
    for start in range(len(edges)):
        stack = [] if start in colour else [start]
        if stack:
            colour[start] = 0
        while stack:
            k = stack.pop()
            for end in (("s", edges[k][0]), ("t", edges[k][1])):
                for other in by_end[end]:
                    if other not in colour:
                        colour[other] = 1 - colour[k]
                        stack.append(other)
    assert all(len({colour[k] for k in ks}) == len(ks) for ks in by_end.values())
    return [colour[k] for k in range(len(edges))]


def make_plan(mesh, count):
    rows, cols = mesh.shape["row"], mesh.shape["col"]
    assert count == rows and count == 2 * cols
    units = list_units(count)
    hosts = choose_hosts(mesh, units, count, cols)
    host = {}
    for unit, device in zip(units, hosts):
        for block in unit:
            host[block] = device
    devices = rows * cols
    table = np.zeros((devices, 16), np.int32)
    gather = [[], []]
    for unit, device in zip(units, hosts):
        for s, (i, j) in enumerate(unit):
            owner = i * cols + j // 2
            gather[s].append((owner, device))
            table[device, 2 * s : 2 * s + 2] = (i, j)
        table[device, 4] = int(unit[0][0] == unit[0][1])
    table[:, 9:13] = -1
    halo = []
    for s in range(2):
        moves = [
            (i, j, k)
            for i in range(count)
            for j in range(count)
            if slot_of(i, j) == s
            for k in (i - 1, i + 1)
            if 0 <= k < count
        ]
        edges = [(host[i, j], host[k, j]) for i, j, k in moves]
        colours = two_colours(edges)
        for colour in range(2):
            number = len(halo)
            halo.append([e for e, c in zip(edges, colours) if c == colour])
            for (i, j, k), (_, target), c in zip(moves, edges, colours):
                if c == colour:
                    table[target, 5 + number] = i
                    table[target, 9 + number] = slot_of(k, j)
    return table, gather, halo


DOT = functools.partial(lax.dot_general, preferred_element_type=jnp.float32)
MATMUL = (((1,), (0,)), ((), ()))


def split(value):
    high = value.astype(jnp.bfloat16)
    low = (value - high.astype(jnp.float32)).astype(jnp.bfloat16)
    return high, low


def constants_kernel(fock_tiles, over_tiles, fock, over, fock_left, over_left, over_right):
    size = fock.shape[0]
    tiles = fock_tiles.shape[0]
    tile = size // tiles
    for a in range(tiles):
        for b in range(tiles):
            rows, cols = pl.ds(a * tile, tile), pl.ds(b * tile, tile)
            high, low = split(fock[rows, cols] * fock_tiles[a, b].astype(jnp.float32))
            for part, value in enumerate((high, high, low)):
                fock_left[rows, pl.ds(part * size + b * tile, tile)] = value
            high, low = split(over[rows, cols] * over_tiles[a, b].astype(jnp.float32))
            for part, value in enumerate((high, high, low)):
                over_left[rows, pl.ds(part * size + b * tile, tile)] = value
            for part, value in enumerate((high, high, low)):
                over_right[pl.ds(part * size + a * tile, tile), cols] = value


PIECE = 16


def pieces(size, begin=0):
    return [pl.ds(begin + n * PIECE, PIECE) for n in range(size // PIECE)]


def three_pass(wide, tall, left):
    size = min(wide.shape[1], tall.shape[0]) // 2
    first = DOT(wide[:, pl.ds(0, 2 * size)], tall[pl.ds(0, 2 * size), :], MATMUL)
    if left:
        return first + DOT(wide[:, pl.ds(2 * size, size)], tall[pl.ds(0, size), :], MATMUL)
    return first + DOT(wide[:, pl.ds(0, size)], tall[pl.ds(2 * size, size), :], MATMUL)


def first_slot():
    i, j = lax.axis_index("row"), lax.axis_index("col") * 2
    return (i + (i > j).astype(jnp.int32)) % 2


def pick_masked_kernel(domain, blocks, out0, out1, near, sems):
    size = blocks.shape[1]
    tiles = domain.shape[1]
    tile = size // tiles
    first = first_slot()
    slots, outs = (first, 1 - first), (out0, out1)
    body = pl.ds(0, size)
    into = [pltpu.make_async_copy(blocks.at[slots[s]], near.at[s, body], sems.at[s]) for s in range(2)]
    back = [pltpu.make_async_copy(near.at[s], outs[s], sems.at[2 + s]) for s in range(2)]
    for copy in into:
        copy.start()
    top = lax.broadcasted_iota(jnp.int32, (PAD, tile), 0) == 0
    for s in range(2):
        for t in range(tiles):
            value = domain[slots[s], t].astype(jnp.float32)
            near[s, pl.ds(size, PAD), pl.ds(t * tile, tile)] = jnp.where(top, value, 0.0)
    for s in range(2):
        into[s].wait()
        back[s].start()
    for copy in back:
        copy.wait()


def own_kernel(x0, x1, fock_left, out, stack):
    size = x0.shape[0]
    for s, x in enumerate((x0, x1)):
        for part in pieces(size):
            high, low = split(x[part, :])
            stack[part, pl.ds(s * size, size)] = high
            stack[pl.ds(size + part.start, PIECE), pl.ds(s * size, size)] = low
    out[...] = three_pass(fock_left, stack, True)


def scale_kernel(table, occ, e_col, e_row, scale):
    for s in range(2):
        i, j = table[2 * s], table[2 * s + 1]
        scale[s] = 1.0 / (e_col[...] + e_row[...] - occ[i, i] - occ[j, j])


def update_kernel(
    table, occ, pattern, x0, x1, r0, r1, r2, r3, own, over_left, over_right, scale, k0, k1,
    y0, y1, near, own_v, left_v, right_v, scale_v, k_v, stack, left, half, g, near_sems, sems,
):
    size = x0.shape[0]
    chunks = near_sems.shape[0]
    rows = size // chunks
    blocks = (x0, x1, r0, r1, r2, r3)

    def near_copy(n, b):
        part = pl.ds(n * rows, rows)
        return pltpu.make_async_copy(blocks[b].at[part], near.at[b, part], near_sems.at[n, b])

    sources = (over_left, own, over_right, scale, k0, k1)
    targets = (left_v, own_v, right_v, scale_v, k_v.at[0], k_v.at[1])
    others = [pltpu.make_async_copy(a, b, sems.at[n]) for n, (a, b) in enumerate(zip(sources, targets))]
    for n in range(chunks):
        for b in range(len(blocks)):
            near_copy(n, b).start()
    for copy in others:
        copy.start()

    def couple(i, k):
        return occ[i, k] * pattern[i, k].astype(jnp.float32)

    own_c, halo_c = [], []
    for s in range(2):
        i = table[2 * s]
        own_c.append(couple(i, i))
        halo_c.append([jnp.where(table[9 + k] == s, couple(i, table[5 + k]), 0.0) for k in range(4)])
    for n in range(chunks):
        for b in range(len(blocks)):
            near_copy(n, b).wait()
        for part in pieces(rows, n * rows):
            values = [near[b, part, :] for b in range(len(blocks))]
            for s in range(2):
                value = own_c[s] * values[s]
                for k in range(4):
                    value += halo_c[s][k] * values[2 + k]
                high, low = split(value)
                stack[part, pl.ds(s * size, size)] = high
                stack[pl.ds(size + part.start, PIECE), pl.ds(s * size, size)] = low
    others[0].wait()
    half[...] = three_pass(left_v, stack, True)
    others[1].wait()
    for s in range(2):
        for part in pieces(size):
            cols = pl.ds(s * size, size)
            high, low = split(own_v[part, cols] - half[part, cols])
            rows_s = pl.ds(s * size + part.start, PIECE)
            left[rows_s, pl.ds(0, size)] = high
            left[rows_s, pl.ds(size, size)] = low
    others[2].wait()
    g[...] = three_pass(left, right_v, False)
    for copy in others[3:]:
        copy.wait()
    other = 1 - table[4]
    tile = min(size, 128)
    for s, y in enumerate((y0, y1)):
        base = (other if s == 0 else 1 - other) * size
        mask = k_v[s, pl.ds(size, PAD), :]
        for a in range(0, size, tile):
            mask_rows = DOT(mask[:, a : a + tile], mask, (((0,), (0,)), ((), ())))
            for b in range(0, size, tile):
                rows_a, cols_b = pl.ds(a, tile), pl.ds(b, tile)
                mirror = g[pl.ds(pl.multiple_of(base + b, tile), tile), rows_a].T
                total = k_v[s, rows_a, cols_b] + g[pl.ds(s * size + a, tile), cols_b] + mirror
                factor = mask_rows[:, b : b + tile] * scale_v[s, rows_a, cols_b]
                y[rows_a, cols_b] = near[s, rows_a, cols_b] - factor * total


SMEM = functools.partial(pl.BlockSpec, memory_space=pltpu.SMEM)
VMEM = functools.partial(pl.BlockSpec, memory_space=pltpu.VMEM)
ANY = functools.partial(pl.BlockSpec, memory_space=pl.ANY)


def constants(fock_tiles, over_tiles, fock, over):
    size = fock.shape[0]
    wide = jax.ShapeDtypeStruct((size, 3 * size), jnp.bfloat16)
    return pl.pallas_call(
        constants_kernel,
        in_specs=[SMEM(), SMEM(), VMEM(), VMEM()],
        out_specs=[VMEM()] * 3,
        out_shape=[wide, wide, jax.ShapeDtypeStruct((3 * size, size), jnp.bfloat16)],
    )(fock_tiles, over_tiles, fock, over)


def pick_masked(blocks, domain):
    size = blocks.shape[1]
    block = jax.ShapeDtypeStruct((size + PAD, size), blocks.dtype)
    return pl.pallas_call(
        pick_masked_kernel,
        in_specs=[SMEM(), ANY()],
        out_specs=[ANY()] * 2,
        out_shape=[block] * 2,
        scratch_shapes=[pltpu.VMEM((2, size + PAD, size), jnp.float32), pltpu.SemaphoreType.DMA((4,))],
    )(domain, blocks)


def own_part(x, fock_left):
    size = x[0].shape[0]
    return pl.pallas_call(
        own_kernel,
        in_specs=[VMEM()] * 3,
        out_specs=VMEM(),
        out_shape=jax.ShapeDtypeStruct((size, 2 * size), jnp.float32),
        scratch_shapes=[pltpu.VMEM((2 * size, 2 * size), jnp.bfloat16)],
    )(*x, fock_left)


def scale_part(table, occ, e_col, e_row):
    size = e_col.shape[0]
    return pl.pallas_call(
        scale_kernel,
        in_specs=[SMEM()] * 2 + [VMEM()] * 2,
        out_specs=VMEM(),
        out_shape=jax.ShapeDtypeStruct((2, size, size), jnp.float32),
    )(table, occ, e_col, e_row)


def update(table, occ, pattern, x, halo, own, over_left, over_right, scale, k):
    size = x[0].shape[0]
    block = jax.ShapeDtypeStruct((size, size), jnp.float32)
    chunks = 3
    return pl.pallas_call(
        update_kernel,
        in_specs=[SMEM()] * 3 + [ANY()] * 12,
        out_specs=[VMEM()] * 2,
        out_shape=[block, block],
        scratch_shapes=[
            pltpu.VMEM((6, size, size), jnp.float32),
            pltpu.VMEM(own.shape, jnp.float32),
            pltpu.VMEM(over_left.shape, jnp.bfloat16),
            pltpu.VMEM(over_right.shape, jnp.bfloat16),
            pltpu.VMEM(scale.shape, jnp.float32),
            pltpu.VMEM((2, *k[0].shape), jnp.float32),
            pltpu.VMEM((2 * size, 2 * size), jnp.bfloat16),
            pltpu.VMEM((2 * size, 2 * size), jnp.bfloat16),
            pltpu.VMEM((size, 2 * size), jnp.float32),
            pltpu.VMEM((2 * size, size), jnp.float32),
            pltpu.SemaphoreType.DMA((chunks, 6)),
            pltpu.SemaphoreType.DMA((6,)),
        ],
    )(table, occ, pattern, *x, *halo, own, over_left, over_right, scale, *k)


def solution(mesh):
    def shards(amplitudes, exchange_ints, fock, over, occ, energy, fock_tiles, over_tiles, pattern, domain):
        count = occ.shape[0]
        assert amplitudes.shape[:2] == (1, 2)
        table, gather, halo = make_plan(mesh, count)
        device = lax.axis_index("row") * mesh.shape["col"] + lax.axis_index("col")
        table = lax.dynamic_index_in_dim(jnp.asarray(table), device, keepdims=False)
        straight = first_slot() == 0

        def by_slot(a, b):
            return jnp.where(straight, a, b), jnp.where(straight, b, a)

        own_x = by_slot(amplitudes[0, 0], amplitudes[0, 1])
        x = [lax.ppermute(value, AXES, moves) for value, moves in zip(own_x, gather)]
        integrals, own_x = lax.optimization_barrier((exchange_ints, own_x))
        own_k = pick_masked(integrals[0], domain[0])
        k = [lax.ppermute(value, AXES, moves) for value, moves in zip(own_k, gather)]
        scale = scale_part(table, occ, energy[:, None], energy[None, :])
        ready = (constants(fock_tiles, over_tiles, fock, over), scale, table)
        x[0], ready = lax.optimization_barrier((x[0], ready))
        (fock_left, over_left, over_right), scale, table = ready
        for _ in range(ITERS):
            nearby = [lax.ppermute(x[n // 2], AXES, moves) for n, moves in enumerate(halo)]
            own = own_part(x, fock_left)
            x = update(table, occ, pattern, x, nearby, own, over_left, over_right, scale, k)
        back = [
            lax.ppermute(value, AXES, [(target, source) for source, target in moves])
            for value, moves in zip(x, gather)
        ]
        return jnp.stack(by_slot(*back))[None]

    blocks = P("row", "col", None, None)
    in_specs = (blocks, blocks, P(), P(), P(), P(), P(), P(), P(), P("row", "col", None))
    return jax.shard_map(shards, mesh=mesh, in_specs=in_specs, out_specs=blocks, check_vma=False)
```

```python
import functools

import jax
import jax.numpy as jnp
import numpy as np
from jax import lax
from jax.experimental import pallas as pl
from jax.experimental.pallas import tpu as pltpu
from jax.sharding import PartitionSpec as P

ITERS = 2
AXES = ("row", "col")
PAD = 8


def slot_of(i, j):
    if i == j:
        return i % 2
    return (i + j + (i > j)) % 2


def list_units(count):
    units = [((i, j), (j, i)) for i in range(count) for j in range(i + 1, count)]
    units += [((i, i), (i + 1, i + 1)) for i in range(0, count, 2)]
    return [tuple(sorted(unit, key=lambda block: slot_of(*block))) for unit in units]


def first_hosts(units, cols):
    hosts = []
    for unit in units:
        i, j = min(unit[0], unit[1])
        if unit[0][0] == unit[0][1]:
            hosts.append((i + 1) * cols + i // 2)
        elif i // 2 == j // 2:
            hosts.append(i * cols + j // 2)
        elif (i + j) % 2 == 0:
            hosts.append(i * cols + j // 2)
        else:
            hosts.append(j * cols + i // 2)
    return hosts


def chip_coords(mesh, cols):
    devices = list(mesh.devices.flat)
    if all(getattr(d, "coords", None) is not None for d in devices):
        return [tuple(d.coords) for d in devices]
    return [(k % cols // 2, k // cols, 0) for k in range(len(devices))]


def route_matrix(chips):
    index = {chip: k for k, chip in enumerate(chips)}
    links = {}
    rows = []
    for a in chips:
        for b in chips:
            here, path = list(a), []
            for axis in (2, 0, 1):
                while here[axis] != b[axis]:
                    there = list(here)
                    there[axis] += 1 if b[axis] > here[axis] else -1
                    if tuple(there) not in index:
                        return None
                    path.append(links.setdefault((tuple(here), tuple(there)), len(links)))
                    here = there
            rows.append(path)
    matrix = np.zeros((len(rows), max(1, len(links))), np.float32)
    for k, path in enumerate(rows):
        matrix[k, path] = 1.0
    return matrix


def choose_hosts(mesh, units, count, cols):
    hosts = first_hosts(units, cols)
    coords = chip_coords(mesh, cols)
    chips = sorted(set(coords))
    if len(chips) > 32:
        return hosts
    routes = route_matrix(chips)
    if routes is None:
        return hosts
    number = len(chips)
    chip_of_device = np.array([chips.index(c) for c in coords])
    block_unit = np.zeros((count, count), np.int64)
    for u, unit in enumerate(units):
        for i, j in unit:
            block_unit[i, j] = u
    owner = np.array([[chip_of_device[i * cols + j // 2] for j in range(count)] for i in range(count)])
    up = np.concatenate([block_unit[:-1].ravel(), block_unit[1:].ravel()])
    down = np.concatenate([block_unit[1:].ravel(), block_unit[:-1].ravel()])
    flat_unit, flat_owner = block_unit.ravel(), owner.ravel()
    pairs = number * number

    chains, steps = 32, 10000
    draw = np.random.RandomState(78)
    offset = (np.arange(chains) * 3 * pairs)[:, None]

    def price(hosts):
        at = chip_of_device[hosts]
        here = at[:, flat_unit]
        keys = [flat_owner * number + here, pairs + here * number + flat_owner, 2 * pairs + at[:, up] * number + at[:, down]]
        keys = np.concatenate(keys, axis=1) + offset
        flows = np.bincount(keys.ravel(), minlength=3 * pairs * chains).astype(np.float32)
        loads = (flows.reshape(-1, pairs) @ routes).reshape(chains, 3, -1)
        there, back, halo = loads[:, 0], loads[:, 1], loads[:, 2]
        peak = there.max(1) + back.max(1) + 2.0 * halo.max(1) + 0.3 * (halo + 2.0 * there).max(1)
        return peak + 0.01 * (loads * loads).sum((1, 2))

    current = np.tile(np.array(hosts), (chains, 1))
    cost = price(current)
    best_cost, best = cost.min(), current[cost.argmin()].copy()
    each = np.arange(chains)
    for step in range(steps):
        heat = 1.5 * 0.02 ** (step / steps)
        a, b = draw.randint(len(units), size=(2, chains))
        trial = current.copy()
        trial[each, a], trial[each, b] = current[each, b], current[each, a]
        trial_cost = price(trial)
        take = (trial_cost <= cost) | (np.exp(np.minimum(0.0, (cost - trial_cost) / heat)) > draw.random_sample(chains))
        current[take], cost[take] = trial[take], trial_cost[take]
        if cost.min() < best_cost:
            best_cost, best = cost.min(), current[cost.argmin()].copy()
    return [int(h) for h in best]


def two_colours(edges):
    by_end = {}
    for k, (source, target) in enumerate(edges):
        by_end.setdefault(("s", source), []).append(k)
        by_end.setdefault(("t", target), []).append(k)
    colour = {}
    for start in range(len(edges)):
        stack = [] if start in colour else [start]
        if stack:
            colour[start] = 0
        while stack:
            k = stack.pop()
            for end in (("s", edges[k][0]), ("t", edges[k][1])):
                for other in by_end[end]:
                    if other not in colour:
                        colour[other] = 1 - colour[k]
                        stack.append(other)
    assert all(len({colour[k] for k in ks}) == len(ks) for ks in by_end.values())
    return [colour[k] for k in range(len(edges))]


def make_plan(mesh, count):
    rows, cols = mesh.shape["row"], mesh.shape["col"]
    assert count == rows and count == 2 * cols
    units = list_units(count)
    hosts = choose_hosts(mesh, units, count, cols)
    host = {}
    for unit, device in zip(units, hosts):
        for block in unit:
            host[block] = device
    devices = rows * cols
    table = np.zeros((devices, 16), np.int32)
    gather = [[], []]
    for unit, device in zip(units, hosts):
        for s, (i, j) in enumerate(unit):
            owner = i * cols + j // 2
            gather[s].append((owner, device))
            table[device, 2 * s : 2 * s + 2] = (i, j)
        table[device, 4] = int(unit[0][0] == unit[0][1])
    table[:, 6::2] = -1
    halo = []
    for s in range(2):
        moves = [
            (i, j, k)
            for i in range(count)
            for j in range(count)
            if slot_of(i, j) == s
            for k in (i - 1, i + 1)
            if 0 <= k < count
        ]
        edges = [(host[i, j], host[k, j]) for i, j, k in moves]
        colours = two_colours(edges)
        for colour in range(2):
            number = len(halo)
            halo.append([e for e, c in zip(edges, colours) if c == colour])
            for (i, j, k), (_, target), c in zip(moves, edges, colours):
                if c == colour:
                    place = 5 + 4 * slot_of(k, j)
                    place += 2 * (table[target, place + 1] >= 0)
                    table[target, place : place + 2] = (number, i)
    return table, gather, halo


DOT = functools.partial(lax.dot_general, preferred_element_type=jnp.float32)
MATMUL = (((1,), (0,)), ((), ()))


def split(value):
    high = value.astype(jnp.bfloat16)
    low = (value - high.astype(jnp.float32)).astype(jnp.bfloat16)
    return high, low


def constants_kernel(fock_tiles, over_tiles, fock, over, fock_left, over_left, over_right):
    size = fock.shape[0]
    tiles = fock_tiles.shape[0]
    tile = size // tiles
    for a in range(tiles):
        for b in range(tiles):
            rows, cols = pl.ds(a * tile, tile), pl.ds(b * tile, tile)
            high, low = split(fock[rows, cols] * fock_tiles[a, b].astype(jnp.float32))
            for part, value in enumerate((high, high, low)):
                fock_left[rows, pl.ds(part * size + b * tile, tile)] = value
            high, low = split(over[rows, cols] * over_tiles[a, b].astype(jnp.float32))
            for part, value in enumerate((high, high, low)):
                over_left[rows, pl.ds(part * size + b * tile, tile)] = value
            for part, value in enumerate((high, high, low)):
                over_right[pl.ds(part * size + a * tile, tile), cols] = value


PIECE = 16


def pieces(size, begin=0):
    return [pl.ds(begin + n * PIECE, PIECE) for n in range(size // PIECE)]


def three_pass(wide, tall, left):
    size = min(wide.shape[1], tall.shape[0]) // 2
    first = DOT(wide[:, pl.ds(0, 2 * size)], tall[pl.ds(0, 2 * size), :], MATMUL)
    if left:
        return first + DOT(wide[:, pl.ds(2 * size, size)], tall[pl.ds(0, size), :], MATMUL)
    return first + DOT(wide[:, pl.ds(0, size)], tall[pl.ds(2 * size, size), :], MATMUL)


def first_slot():
    i, j = lax.axis_index("row"), lax.axis_index("col") * 2
    return (i + (i > j).astype(jnp.int32)) % 2


def pick_masked_kernel(domain, blocks, out0, out1, near, sems):
    size = blocks.shape[1]
    tiles = domain.shape[1]
    tile = size // tiles
    first = first_slot()
    slots, outs = (first, 1 - first), (out0, out1)
    body = pl.ds(0, size)
    into = [pltpu.make_async_copy(blocks.at[slots[s]], near.at[s, body], sems.at[s]) for s in range(2)]
    back = [pltpu.make_async_copy(near.at[s], outs[s], sems.at[2 + s]) for s in range(2)]
    for copy in into:
        copy.start()
    top = lax.broadcasted_iota(jnp.int32, (PAD, tile), 0) == 0
    for s in range(2):
        for t in range(tiles):
            value = domain[slots[s], t].astype(jnp.float32)
            near[s, pl.ds(size, PAD), pl.ds(t * tile, tile)] = jnp.where(top, value, 0.0)
    for s in range(2):
        into[s].wait()
        back[s].start()
    for copy in back:
        copy.wait()


def couple(occ, pattern, i, k):
    return occ[i, k] * pattern[i, k].astype(jnp.float32)


def own_kernel(table, occ, pattern, x0, x1, fock_left, over_left, out, stack):
    size = x0.shape[0]
    for s, x in enumerate((x0, x1)):
        for part in pieces(size):
            high, low = split(x[part, :])
            stack[part, pl.ds(s * size, size)] = high
            stack[pl.ds(size + part.start, PIECE), pl.ds(s * size, size)] = low
    out[...] = three_pass(fock_left, stack, True)
    over_x = three_pass(over_left, stack, True)
    for s in range(2):
        i, cols = table[2 * s], pl.ds(s * size, size)
        out[:, cols] = out[:, cols] - couple(occ, pattern, i, i) * over_x[:, s * size : (s + 1) * size]


def scale_kernel(table, occ, e_col, e_row, scale):
    for s in range(2):
        i, j = table[2 * s], table[2 * s + 1]
        scale[s] = 1.0 / (e_col[...] + e_row[...] - occ[i, i] - occ[j, j])


def update_kernel(
    table, occ, pattern, x0, x1, r0, r1, r2, r3, own, over_left, over_right, scale, k0, k1,
    y0, y1, stack, left, half, g,
):
    size = x0.shape[0]
    halo, x, k, y = (r0, r1, r2, r3), (x0, x1), (k0, k1), (y0, y1)
    coefs = []
    for s in range(2):
        factors = [couple(occ, pattern, table[2 * s], jnp.maximum(table[place + 1], 0)) for place in (5 + 4 * s, 7 + 4 * s)]
        coefs.append([0.0] * len(halo))
        for place, factor in zip((5 + 4 * s, 7 + 4 * s), factors):
            for number in range(len(halo)):
                here = (table[place] == number) & (table[place + 1] >= 0)
                coefs[s][number] += jnp.where(here, factor, 0.0)
    for part in pieces(size):
        for s in range(2):
            value = 0.0
            for number, r in enumerate(halo):
                value += coefs[s][number] * r[part, :]
            high, low = split(value)
            stack[part, pl.ds(s * size, size)] = high
            stack[pl.ds(size + part.start, PIECE), pl.ds(s * size, size)] = low
    half[...] = three_pass(over_left, stack, True)
    for s in range(2):
        for part in pieces(size):
            cols = pl.ds(s * size, size)
            high, low = split(own[part, cols] - half[part, cols])
            rows_s = pl.ds(s * size + part.start, PIECE)
            left[rows_s, pl.ds(0, size)] = high
            left[rows_s, pl.ds(size, size)] = low
    g[...] = three_pass(left, over_right, False)
    other = 1 - table[4]
    tile = min(size, 128)
    for s in range(2):
        base = (other if s == 0 else 1 - other) * size
        mask = k[s][pl.ds(size, PAD), :]
        for a in range(0, size, tile):
            mask_rows = DOT(mask[:, a : a + tile], mask, (((0,), (0,)), ((), ())))
            for b in range(0, size, tile):
                rows_a, cols_b = pl.ds(a, tile), pl.ds(b, tile)
                mirror = g[pl.ds(pl.multiple_of(base + b, tile), tile), rows_a].T
                total = k[s][rows_a, cols_b] + g[pl.ds(s * size + a, tile), cols_b] + mirror
                factor = mask_rows[:, b : b + tile] * scale[s, rows_a, cols_b]
                y[s][rows_a, cols_b] = x[s][rows_a, cols_b] - factor * total


SMEM = functools.partial(pl.BlockSpec, memory_space=pltpu.SMEM)
VMEM = functools.partial(pl.BlockSpec, memory_space=pltpu.VMEM)
ANY = functools.partial(pl.BlockSpec, memory_space=pl.ANY)
LIMIT = pltpu.CompilerParams(vmem_limit_bytes=24 * 2**20)


def constants(fock_tiles, over_tiles, fock, over):
    size = fock.shape[0]
    wide = pltpu.VMEM((size, 3 * size), jnp.bfloat16)
    return pl.pallas_call(
        constants_kernel,
        compiler_params=LIMIT,
        in_specs=[SMEM(), SMEM(), VMEM(), VMEM()],
        out_specs=[VMEM()] * 3,
        out_shape=[wide, wide, pltpu.VMEM((3 * size, size), jnp.bfloat16)],
    )(fock_tiles, over_tiles, fock, over)


def pick_masked(blocks, domain):
    size = blocks.shape[1]
    block = jax.ShapeDtypeStruct((size + PAD, size), blocks.dtype)
    return pl.pallas_call(
        pick_masked_kernel,
        compiler_params=LIMIT,
        in_specs=[SMEM(), ANY()],
        out_specs=[ANY()] * 2,
        out_shape=[block] * 2,
        scratch_shapes=[pltpu.VMEM((2, size + PAD, size), jnp.float32), pltpu.SemaphoreType.DMA((4,))],
    )(domain, blocks)


def own_part(table, occ, pattern, x, fock_left, over_left):
    size = x[0].shape[0]
    return pl.pallas_call(
        own_kernel,
        compiler_params=LIMIT,
        in_specs=[SMEM()] * 3 + [VMEM()] * 4,
        out_specs=VMEM(),
        out_shape=pltpu.VMEM((size, 2 * size), jnp.float32),
        scratch_shapes=[pltpu.VMEM((2 * size, 2 * size), jnp.bfloat16)],
    )(table, occ, pattern, *x, fock_left, over_left)


def scale_part(table, occ, e_col, e_row):
    size = e_col.shape[0]
    return pl.pallas_call(
        scale_kernel,
        compiler_params=LIMIT,
        in_specs=[SMEM()] * 2 + [VMEM()] * 2,
        out_specs=VMEM(),
        out_shape=pltpu.VMEM((2, size, size), jnp.float32),
    )(table, occ, e_col, e_row)


def update(table, occ, pattern, x, halo, own, over_left, over_right, scale, k):
    size = x[0].shape[0]
    block = pltpu.VMEM((size, size), jnp.float32)
    return pl.pallas_call(
        update_kernel,
        compiler_params=LIMIT,
        in_specs=[SMEM()] * 3 + [VMEM()] * 12,
        out_specs=[VMEM()] * 2,
        out_shape=[block, block],
        scratch_shapes=[
            pltpu.VMEM((2 * size, 2 * size), jnp.bfloat16),
            pltpu.VMEM((2 * size, 2 * size), jnp.bfloat16),
            pltpu.VMEM((size, 2 * size), jnp.float32),
            pltpu.VMEM((2 * size, size), jnp.float32),
        ],
    )(table, occ, pattern, *x, *halo, own, over_left, over_right, scale, *k)


def send(value, moves):
    return pltpu.with_memory_space_constraint(lax.ppermute(value, AXES, moves), pltpu.VMEM)


def solution(mesh):
    def shards(amplitudes, exchange_ints, fock, over, occ, energy, fock_tiles, over_tiles, pattern, domain):
        count = occ.shape[0]
        assert amplitudes.shape[:2] == (1, 2)
        table, gather, halo = make_plan(mesh, count)
        device = lax.axis_index("row") * mesh.shape["col"] + lax.axis_index("col")
        table = lax.dynamic_index_in_dim(jnp.asarray(table), device, keepdims=False)
        straight = first_slot() == 0

        def by_slot(a, b):
            return jnp.where(straight, a, b), jnp.where(straight, b, a)

        first = first_slot()
        own_x = [lax.dynamic_index_in_dim(amplitudes[0], first, keepdims=False)]
        own_x[0], second = lax.optimization_barrier((own_x[0], 1 - first))
        own_x.append(lax.dynamic_index_in_dim(amplitudes[0], second, keepdims=False))
        x = [send(value, moves) for value, moves in zip(own_x, gather)]
        integrals, own_x = lax.optimization_barrier((exchange_ints, own_x))
        own_k = pick_masked(integrals[0], domain[0])
        k = [send(value, moves) for value, moves in zip(own_k, gather)]
        scale = scale_part(table, occ, energy[:, None], energy[None, :])
        ready = (constants(fock_tiles, over_tiles, fock, over), scale, table)
        x[0], ready = lax.optimization_barrier((x[0], ready))
        (fock_left, over_left, over_right), scale, table = ready
        for _ in range(ITERS):
            nearby = [send(x[n // 2], moves) for n, moves in enumerate(halo)]
            own = own_part(table, occ, pattern, x, fock_left, over_left)
            x = update(table, occ, pattern, x, nearby, own, over_left, over_right, scale, k)
        back = [
            lax.ppermute(value, AXES, [(target, source) for source, target in moves])
            for value, moves in zip(x, gather)
        ]
        return jnp.stack(by_slot(*back))[None]

    blocks = P("row", "col", None, None)
    in_specs = (blocks, blocks, P(), P(), P(), P(), P(), P(), P(), P("row", "col", None))
    return jax.shard_map(shards, mesh=mesh, in_specs=in_specs, out_specs=blocks, check_vma=False)
```

```python
import functools

import jax
import jax.numpy as jnp
import numpy as np
from jax import lax
from jax.experimental import pallas as pl
from jax.experimental.pallas import tpu as pltpu
from jax.sharding import PartitionSpec as P

ITERS = 2
AXES = ("row", "col")
PAD = 8


def slot_of(i, j):
    if i == j:
        return i % 2
    return (i + j + (i > j)) % 2


def list_units(count):
    units = [((i, j), (j, i)) for i in range(count) for j in range(i + 1, count)]
    units += [((i, i), (i + 1, i + 1)) for i in range(0, count, 2)]
    return [tuple(sorted(unit, key=lambda block: slot_of(*block))) for unit in units]


def first_hosts(units, cols):
    hosts = []
    for unit in units:
        i, j = min(unit[0], unit[1])
        if unit[0][0] == unit[0][1]:
            hosts.append((i + 1) * cols + i // 2)
        elif i // 2 == j // 2:
            hosts.append(i * cols + j // 2)
        elif (i + j) % 2 == 0:
            hosts.append(i * cols + j // 2)
        else:
            hosts.append(j * cols + i // 2)
    return hosts


def chip_coords(mesh, cols):
    devices = list(mesh.devices.flat)
    if all(getattr(d, "coords", None) is not None for d in devices):
        return [tuple(d.coords) for d in devices]
    return [(k % cols // 2, k // cols, 0) for k in range(len(devices))]


def route_matrix(chips):
    index = {chip: k for k, chip in enumerate(chips)}
    links = {}
    rows = []
    for a in chips:
        for b in chips:
            here, path = list(a), []
            for axis in (2, 0, 1):
                while here[axis] != b[axis]:
                    there = list(here)
                    there[axis] += 1 if b[axis] > here[axis] else -1
                    if tuple(there) not in index:
                        return None
                    path.append(links.setdefault((tuple(here), tuple(there)), len(links)))
                    here = there
            rows.append(path)
    matrix = np.zeros((len(rows), max(1, len(links))), np.float32)
    for k, path in enumerate(rows):
        matrix[k, path] = 1.0
    return matrix


def choose_hosts(mesh, units, count, cols):
    hosts = first_hosts(units, cols)
    coords = chip_coords(mesh, cols)
    chips = sorted(set(coords))
    if len(chips) > 32:
        return hosts
    routes = route_matrix(chips)
    if routes is None:
        return hosts
    number = len(chips)
    chip_of_device = np.array([chips.index(c) for c in coords])
    block_unit = np.zeros((count, count), np.int64)
    for u, unit in enumerate(units):
        for i, j in unit:
            block_unit[i, j] = u
    owner = np.array([[chip_of_device[i * cols + j // 2] for j in range(count)] for i in range(count)])
    up = np.concatenate([block_unit[:-1].ravel(), block_unit[1:].ravel()])
    down = np.concatenate([block_unit[1:].ravel(), block_unit[:-1].ravel()])
    flat_unit, flat_owner = block_unit.ravel(), owner.ravel()
    pairs = number * number

    chains, steps = 32, 10000
    draw = np.random.RandomState(78)
    offset = (np.arange(chains) * 3 * pairs)[:, None]

    def price(hosts):
        at = chip_of_device[hosts]
        here = at[:, flat_unit]
        keys = [flat_owner * number + here, pairs + here * number + flat_owner, 2 * pairs + at[:, up] * number + at[:, down]]
        keys = np.concatenate(keys, axis=1) + offset
        flows = np.bincount(keys.ravel(), minlength=3 * pairs * chains).astype(np.float32)
        loads = (flows.reshape(-1, pairs) @ routes).reshape(chains, 3, -1)
        there, back, halo = loads[:, 0], loads[:, 1], loads[:, 2]
        peak = there.max(1) + back.max(1) + 2.0 * halo.max(1) + 0.3 * (halo + 2.0 * there).max(1)
        return peak + 0.01 * (loads * loads).sum((1, 2))

    current = np.tile(np.array(hosts), (chains, 1))
    cost = price(current)
    best_cost, best = cost.min(), current[cost.argmin()].copy()
    each = np.arange(chains)
    for step in range(steps):
        heat = 1.5 * 0.02 ** (step / steps)
        a, b = draw.randint(len(units), size=(2, chains))
        trial = current.copy()
        trial[each, a], trial[each, b] = current[each, b], current[each, a]
        trial_cost = price(trial)
        take = (trial_cost <= cost) | (np.exp(np.minimum(0.0, (cost - trial_cost) / heat)) > draw.random_sample(chains))
        current[take], cost[take] = trial[take], trial_cost[take]
        if cost.min() < best_cost:
            best_cost, best = cost.min(), current[cost.argmin()].copy()
    return [int(h) for h in best]


def two_colours(edges):
    by_end = {}
    for k, (source, target) in enumerate(edges):
        by_end.setdefault(("s", source), []).append(k)
        by_end.setdefault(("t", target), []).append(k)
    colour = {}
    for start in range(len(edges)):
        stack = [] if start in colour else [start]
        if stack:
            colour[start] = 0
        while stack:
            k = stack.pop()
            for end in (("s", edges[k][0]), ("t", edges[k][1])):
                for other in by_end[end]:
                    if other not in colour:
                        colour[other] = 1 - colour[k]
                        stack.append(other)
    assert all(len({colour[k] for k in ks}) == len(ks) for ks in by_end.values())
    return [colour[k] for k in range(len(edges))]


def make_plan(mesh, count):
    rows, cols = mesh.shape["row"], mesh.shape["col"]
    assert count == rows and count == 2 * cols
    units = list_units(count)
    hosts = choose_hosts(mesh, units, count, cols)
    host = {}
    for unit, device in zip(units, hosts):
        for block in unit:
            host[block] = device
    devices = rows * cols
    table = np.zeros((devices, 16), np.int32)
    gather = [[], []]
    for unit, device in zip(units, hosts):
        for s, (i, j) in enumerate(unit):
            owner = i * cols + j // 2
            gather[s].append((owner, device))
            table[device, 2 * s : 2 * s + 2] = (i, j)
        table[device, 4] = int(unit[0][0] == unit[0][1])
    table[:, 6::2] = -1
    halo = []
    for s in range(2):
        moves = [
            (i, j, k)
            for i in range(count)
            for j in range(count)
            if slot_of(i, j) == s
            for k in (i - 1, i + 1)
            if 0 <= k < count
        ]
        edges = [(host[i, j], host[k, j]) for i, j, k in moves]
        colours = two_colours(edges)
        for colour in range(2):
            number = len(halo)
            halo.append([e for e, c in zip(edges, colours) if c == colour])
            for (i, j, k), (_, target), c in zip(moves, edges, colours):
                if c == colour:
                    place = 5 + 4 * slot_of(k, j)
                    place += 2 * (table[target, place + 1] >= 0)
                    table[target, place : place + 2] = (number, i)
    return table, gather, halo


DOT = functools.partial(lax.dot_general, preferred_element_type=jnp.float32)
MATMUL = (((1,), (0,)), ((), ()))


def split(value):
    high = value.astype(jnp.bfloat16)
    low = (value - high.astype(jnp.float32)).astype(jnp.bfloat16)
    return high, low


def constants_kernel(fock_tiles, over_tiles, fock, over, fock_left, over_left, over_right):
    size = fock.shape[0]
    tiles = fock_tiles.shape[0]
    tile = size // tiles
    for a in range(tiles):
        for b in range(tiles):
            rows, cols = pl.ds(a * tile, tile), pl.ds(b * tile, tile)
            high, low = split(fock[rows, cols] * fock_tiles[a, b].astype(jnp.float32))
            for part, value in enumerate((high, high, low)):
                fock_left[rows, pl.ds(part * size + b * tile, tile)] = value
            high, low = split(over[rows, cols] * over_tiles[a, b].astype(jnp.float32))
            for part, value in enumerate((high, high, low)):
                over_left[rows, pl.ds(part * size + b * tile, tile)] = value
            for part, value in enumerate((high, high, low)):
                over_right[pl.ds(part * size + a * tile, tile), cols] = value


PIECE = 16


def pieces(size, begin=0):
    return [pl.ds(begin + n * PIECE, PIECE) for n in range(size // PIECE)]


def three_pass(wide, tall, left):
    size = min(wide.shape[1], tall.shape[0]) // 2
    first = DOT(wide[:, pl.ds(0, 2 * size)], tall[pl.ds(0, 2 * size), :], MATMUL)
    if left:
        return first + DOT(wide[:, pl.ds(2 * size, size)], tall[pl.ds(0, size), :], MATMUL)
    return first + DOT(wide[:, pl.ds(0, size)], tall[pl.ds(2 * size, size), :], MATMUL)


def first_slot():
    i, j = lax.axis_index("row"), lax.axis_index("col") * 2
    return (i + (i > j).astype(jnp.int32)) % 2


def pick_kernel(blocks, out, sem, *, second):
    slot = 1 - first_slot() if second else first_slot()
    copy = pltpu.make_async_copy(blocks.at[slot], out, sem)
    copy.start()
    copy.wait()


def pick_masked_kernel(domain, blocks, out0, out1, sems):
    size = blocks.shape[1]
    tiles = domain.shape[1]
    tile = size // tiles
    first = first_slot()
    slots, outs = (first, 1 - first), (out0, out1)
    body = pl.ds(0, size)
    copies = [pltpu.make_async_copy(blocks.at[slots[s]], outs[s].at[body], sems.at[s]) for s in range(2)]
    for copy in copies:
        copy.start()
    top = lax.broadcasted_iota(jnp.int32, (PAD, tile), 0) == 0
    for s in range(2):
        for t in range(tiles):
            value = domain[slots[s], t].astype(jnp.float32)
            outs[s][pl.ds(size, PAD), pl.ds(t * tile, tile)] = jnp.where(top, value, 0.0)
    for copy in copies:
        copy.wait()


def couple(occ, pattern, i, k):
    return occ[i, k] * pattern[i, k].astype(jnp.float32)


def own_kernel(table, occ, pattern, x0, x1, fock_left, over_left, out, stack):
    size = x0.shape[0]
    for s, x in enumerate((x0, x1)):
        for part in pieces(size):
            high, low = split(x[part, :])
            stack[part, pl.ds(s * size, size)] = high
            stack[pl.ds(size + part.start, PIECE), pl.ds(s * size, size)] = low
    out[...] = three_pass(fock_left, stack, True)
    over_x = three_pass(over_left, stack, True)
    for s in range(2):
        i, cols = table[2 * s], pl.ds(s * size, size)
        out[:, cols] = out[:, cols] - couple(occ, pattern, i, i) * over_x[:, s * size : (s + 1) * size]


def scale_kernel(table, occ, e_col, e_row, scale):
    for s in range(2):
        i, j = table[2 * s], table[2 * s + 1]
        scale[s] = 1.0 / (e_col[...] + e_row[...] - occ[i, i] - occ[j, j])


def update_kernel(
    table, occ, pattern, x0, x1, r0, r1, r2, r3, own, over_left, over_right, scale, k0, k1,
    y0, y1, stack, left, half, g,
):
    size = x0.shape[0]
    halo, x, k, y = (r0, r1, r2, r3), (x0, x1), (k0, k1), (y0, y1)
    coefs = []
    for s in range(2):
        factors = [couple(occ, pattern, table[2 * s], jnp.maximum(table[place + 1], 0)) for place in (5 + 4 * s, 7 + 4 * s)]
        coefs.append([0.0] * len(halo))
        for place, factor in zip((5 + 4 * s, 7 + 4 * s), factors):
            for number in range(len(halo)):
                here = (table[place] == number) & (table[place + 1] >= 0)
                coefs[s][number] += jnp.where(here, factor, 0.0)
    for part in pieces(size):
        for s in range(2):
            value = 0.0
            for number, r in enumerate(halo):
                value += coefs[s][number] * r[part, :]
            high, low = split(value)
            stack[part, pl.ds(s * size, size)] = high
            stack[pl.ds(size + part.start, PIECE), pl.ds(s * size, size)] = low
    half[...] = three_pass(over_left, stack, True)
    for s in range(2):
        for part in pieces(size):
            cols = pl.ds(s * size, size)
            high, low = split(own[part, cols] - half[part, cols])
            rows_s = pl.ds(s * size + part.start, PIECE)
            left[rows_s, pl.ds(0, size)] = high
            left[rows_s, pl.ds(size, size)] = low
    g[...] = three_pass(left, over_right, False)
    other = 1 - table[4]
    tile = min(size, 128)
    for s in range(2):
        base = (other if s == 0 else 1 - other) * size
        mask = k[s][pl.ds(size, PAD), :]
        for a in range(0, size, tile):
            mask_rows = DOT(mask[:, a : a + tile], mask, (((0,), (0,)), ((), ())))
            for b in range(0, size, tile):
                rows_a, cols_b = pl.ds(a, tile), pl.ds(b, tile)
                mirror = g[pl.ds(pl.multiple_of(base + b, tile), tile), rows_a].T
                total = k[s][rows_a, cols_b] + g[pl.ds(s * size + a, tile), cols_b] + mirror
                factor = mask_rows[:, b : b + tile] * scale[s, rows_a, cols_b]
                y[s][rows_a, cols_b] = x[s][rows_a, cols_b] - factor * total


SMEM = functools.partial(pl.BlockSpec, memory_space=pltpu.SMEM)
VMEM = functools.partial(pl.BlockSpec, memory_space=pltpu.VMEM)
ANY = functools.partial(pl.BlockSpec, memory_space=pl.ANY)
LIMIT = pltpu.CompilerParams(vmem_limit_bytes=24 * 2**20)


def constants(fock_tiles, over_tiles, fock, over):
    size = fock.shape[0]
    wide = pltpu.VMEM((size, 3 * size), jnp.bfloat16)
    return pl.pallas_call(
        constants_kernel,
        compiler_params=LIMIT,
        in_specs=[SMEM(), SMEM(), VMEM(), VMEM()],
        out_specs=[VMEM()] * 3,
        out_shape=[wide, wide, pltpu.VMEM((3 * size, size), jnp.bfloat16)],
    )(fock_tiles, over_tiles, fock, over)


def pick(blocks, second):
    return pl.pallas_call(
        functools.partial(pick_kernel, second=second),
        compiler_params=LIMIT,
        in_specs=[ANY()],
        out_specs=VMEM(),
        out_shape=pltpu.VMEM(blocks.shape[1:], blocks.dtype),
        scratch_shapes=[pltpu.SemaphoreType.DMA],
    )(blocks)


def pick_masked(blocks, domain):
    size = blocks.shape[1]
    block = pltpu.VMEM((size + PAD, size), blocks.dtype)
    return pl.pallas_call(
        pick_masked_kernel,
        compiler_params=LIMIT,
        in_specs=[SMEM(), ANY()],
        out_specs=[VMEM()] * 2,
        out_shape=[block] * 2,
        scratch_shapes=[pltpu.SemaphoreType.DMA((2,))],
    )(domain, blocks)


def own_part(table, occ, pattern, x, fock_left, over_left):
    size = x[0].shape[0]
    return pl.pallas_call(
        own_kernel,
        compiler_params=LIMIT,
        in_specs=[SMEM()] * 3 + [VMEM()] * 4,
        out_specs=VMEM(),
        out_shape=pltpu.VMEM((size, 2 * size), jnp.float32),
        scratch_shapes=[pltpu.VMEM((2 * size, 2 * size), jnp.bfloat16)],
    )(table, occ, pattern, *x, fock_left, over_left)


def scale_part(table, occ, e_col, e_row):
    size = e_col.shape[0]
    return pl.pallas_call(
        scale_kernel,
        compiler_params=LIMIT,
        in_specs=[SMEM()] * 2 + [VMEM()] * 2,
        out_specs=VMEM(),
        out_shape=pltpu.VMEM((2, size, size), jnp.float32),
    )(table, occ, e_col, e_row)


def update(table, occ, pattern, x, halo, own, over_left, over_right, scale, k):
    size = x[0].shape[0]
    block = pltpu.VMEM((size, size), jnp.float32)
    return pl.pallas_call(
        update_kernel,
        compiler_params=LIMIT,
        in_specs=[SMEM()] * 3 + [VMEM()] * 12,
        out_specs=[VMEM()] * 2,
        out_shape=[block, block],
        scratch_shapes=[
            pltpu.VMEM((2 * size, 2 * size), jnp.bfloat16),
            pltpu.VMEM((2 * size, 2 * size), jnp.bfloat16),
            pltpu.VMEM((size, 2 * size), jnp.float32),
            pltpu.VMEM((2 * size, size), jnp.float32),
        ],
    )(table, occ, pattern, *x, *halo, own, over_left, over_right, scale, *k)


def send(value, moves):
    value = lax.ppermute(value, AXES, moves)
    return pltpu.with_memory_space_constraint(value, pltpu.VMEM)


def solution(mesh):
    def shards(amplitudes, exchange_ints, fock, over, occ, energy, fock_tiles, over_tiles, pattern, domain):
        count = occ.shape[0]
        assert amplitudes.shape[:2] == (1, 2)
        table, gather, halo = make_plan(mesh, count)
        device = lax.axis_index("row") * mesh.shape["col"] + lax.axis_index("col")
        table = lax.dynamic_index_in_dim(jnp.asarray(table), device, keepdims=False)
        straight = first_slot() == 0

        def by_slot(a, b):
            return jnp.where(straight, a, b), jnp.where(straight, b, a)

        own_x = [pick(amplitudes[0], False)]
        blocks, own_x[0] = lax.optimization_barrier((amplitudes, own_x[0]))
        own_x.append(pick(blocks[0], True))
        x = [send(own_x[n], gather[n]) for n in range(2)]
        integrals, own_x = lax.optimization_barrier((exchange_ints, own_x))
        own_k = pick_masked(integrals[0], domain[0])
        k = [send(own_k[n], gather[n]) for n in range(2)]
        scale = scale_part(table, occ, energy[:, None], energy[None, :])
        ready = (constants(fock_tiles, over_tiles, fock, over), scale, table)
        x[0], ready = lax.optimization_barrier((x[0], ready))
        (fock_left, over_left, over_right), scale, table = ready
        for _ in range(ITERS):
            nearby = [send(x[n // 2], moves) for n, moves in enumerate(halo)]
            own = own_part(table, occ, pattern, x, fock_left, over_left)
            x = update(table, occ, pattern, x, nearby, own, over_left, over_right, scale, k)
        back = [
            lax.ppermute(value, AXES, [(target, source) for source, target in moves])
            for value, moves in zip(x, gather)
        ]
        return jnp.stack(by_slot(*back))[None]

    blocks = P("row", "col", None, None)
    in_specs = (blocks, blocks, P(), P(), P(), P(), P(), P(), P(), P("row", "col", None))
    return jax.shard_map(shards, mesh=mesh, in_specs=in_specs, out_specs=blocks, check_vma=False)
```

```python
import functools

import jax
import jax.numpy as jnp
import numpy as np
from jax import lax
from jax.experimental import pallas as pl
from jax.experimental.pallas import tpu as pltpu
from jax.sharding import PartitionSpec as P

ITERS = 2
AXES = ("row", "col")
PAD = 8


def slot_of(i, j):
    if i == j:
        return i % 2
    return (i + j + (i > j)) % 2


def list_units(count):
    units = [((i, j), (j, i)) for i in range(count) for j in range(i + 1, count)]
    units += [((i, i), (i + 1, i + 1)) for i in range(0, count, 2)]
    return [tuple(sorted(unit, key=lambda block: slot_of(*block))) for unit in units]


def first_hosts(units, cols):
    hosts = []
    for unit in units:
        i, j = min(unit[0], unit[1])
        if unit[0][0] == unit[0][1]:
            hosts.append((i + 1) * cols + i // 2)
        elif i // 2 == j // 2:
            hosts.append(i * cols + j // 2)
        elif (i + j) % 2 == 0:
            hosts.append(i * cols + j // 2)
        else:
            hosts.append(j * cols + i // 2)
    return hosts


def chip_coords(mesh, cols):
    devices = list(mesh.devices.flat)
    if all(getattr(d, "coords", None) is not None for d in devices):
        return [tuple(d.coords) for d in devices]
    return [(k % cols // 2, k // cols, 0) for k in range(len(devices))]


def route_matrix(chips):
    index = {chip: k for k, chip in enumerate(chips)}
    links = {}
    rows = []
    for a in chips:
        for b in chips:
            here, path = list(a), []
            for axis in (2, 0, 1):
                while here[axis] != b[axis]:
                    there = list(here)
                    there[axis] += 1 if b[axis] > here[axis] else -1
                    if tuple(there) not in index:
                        return None
                    path.append(links.setdefault((tuple(here), tuple(there)), len(links)))
                    here = there
            rows.append(path)
    matrix = np.zeros((len(rows), max(1, len(links))), np.float32)
    for k, path in enumerate(rows):
        matrix[k, path] = 1.0
    return matrix


def choose_hosts(mesh, units, count, cols):
    hosts = first_hosts(units, cols)
    coords = chip_coords(mesh, cols)
    chips = sorted(set(coords))
    if len(chips) > 32:
        return hosts
    routes = route_matrix(chips)
    if routes is None:
        return hosts
    number = len(chips)
    chip_of_device = np.array([chips.index(c) for c in coords])
    block_unit = np.zeros((count, count), np.int64)
    for u, unit in enumerate(units):
        for i, j in unit:
            block_unit[i, j] = u
    owner = np.array([[chip_of_device[i * cols + j // 2] for j in range(count)] for i in range(count)])
    up = np.concatenate([block_unit[:-1].ravel(), block_unit[1:].ravel()])
    down = np.concatenate([block_unit[1:].ravel(), block_unit[:-1].ravel()])
    flat_unit, flat_owner = block_unit.ravel(), owner.ravel()
    pairs = number * number

    chains, steps = 32, 10000
    draw = np.random.RandomState(78)
    offset = (np.arange(chains) * 3 * pairs)[:, None]

    def price(hosts):
        at = chip_of_device[hosts]
        here = at[:, flat_unit]
        keys = [flat_owner * number + here, pairs + here * number + flat_owner, 2 * pairs + at[:, up] * number + at[:, down]]
        keys = np.concatenate(keys, axis=1) + offset
        flows = np.bincount(keys.ravel(), minlength=3 * pairs * chains).astype(np.float32)
        loads = (flows.reshape(-1, pairs) @ routes).reshape(chains, 3, -1)
        there, back, halo = loads[:, 0], loads[:, 1], loads[:, 2]
        peak = there.max(1) + back.max(1) + 2.0 * halo.max(1) + 0.3 * (halo + 2.0 * there).max(1)
        return peak + 0.01 * (loads * loads).sum((1, 2))

    current = np.tile(np.array(hosts), (chains, 1))
    cost = price(current)
    best_cost, best = cost.min(), current[cost.argmin()].copy()
    each = np.arange(chains)
    for step in range(steps):
        heat = 1.5 * 0.02 ** (step / steps)
        a, b = draw.randint(len(units), size=(2, chains))
        trial = current.copy()
        trial[each, a], trial[each, b] = current[each, b], current[each, a]
        trial_cost = price(trial)
        take = (trial_cost <= cost) | (np.exp(np.minimum(0.0, (cost - trial_cost) / heat)) > draw.random_sample(chains))
        current[take], cost[take] = trial[take], trial_cost[take]
        if cost.min() < best_cost:
            best_cost, best = cost.min(), current[cost.argmin()].copy()
    hosts = [int(h) for h in best]
    owners = [[i * cols + j // 2 for i, j in unit] for unit in units]
    for a in range(len(units)):
        for b in range(a):
            if chip_of_device[hosts[a]] == chip_of_device[hosts[b]]:
                kept = owners[a].count(hosts[a]) + owners[b].count(hosts[b])
                swapped = owners[a].count(hosts[b]) + owners[b].count(hosts[a])
                if swapped < kept:
                    hosts[a], hosts[b] = hosts[b], hosts[a]
    return hosts


def two_colours(edges):
    by_end = {}
    for k, (source, target) in enumerate(edges):
        by_end.setdefault(("s", source), []).append(k)
        by_end.setdefault(("t", target), []).append(k)
    colour = {}
    for start in range(len(edges)):
        stack = [] if start in colour else [start]
        if stack:
            colour[start] = 0
        while stack:
            k = stack.pop()
            for end in (("s", edges[k][0]), ("t", edges[k][1])):
                for other in by_end[end]:
                    if other not in colour:
                        colour[other] = 1 - colour[k]
                        stack.append(other)
    assert all(len({colour[k] for k in ks}) == len(ks) for ks in by_end.values())
    return [colour[k] for k in range(len(edges))]


def make_plan(mesh, count):
    rows, cols = mesh.shape["row"], mesh.shape["col"]
    assert count == rows and count == 2 * cols
    units = list_units(count)
    hosts = choose_hosts(mesh, units, count, cols)
    host = {}
    for unit, device in zip(units, hosts):
        for block in unit:
            host[block] = device
    devices = rows * cols
    table = np.zeros((devices, 16), np.int32)
    gather = [[], []]
    for unit, device in zip(units, hosts):
        for s, (i, j) in enumerate(unit):
            owner = i * cols + j // 2
            gather[s].append((owner, device))
            table[device, 2 * s : 2 * s + 2] = (i, j)
        table[device, 4] = int(unit[0][0] == unit[0][1])
    table[:, 6::2] = -1
    halo = []
    for s in range(2):
        moves = [
            (i, j, k)
            for i in range(count)
            for j in range(count)
            if slot_of(i, j) == s
            for k in (i - 1, i + 1)
            if 0 <= k < count
        ]
        edges = [(host[i, j], host[k, j]) for i, j, k in moves]
        colours = two_colours(edges)
        for colour in range(2):
            number = len(halo)
            halo.append([e for e, c in zip(edges, colours) if c == colour])
            for (i, j, k), (_, target), c in zip(moves, edges, colours):
                if c == colour:
                    place = 5 + 4 * slot_of(k, j)
                    place += 2 * (table[target, place + 1] >= 0)
                    table[target, place : place + 2] = (number, i)
    return table, gather, halo


DOT = functools.partial(lax.dot_general, preferred_element_type=jnp.float32)
MATMUL = (((1,), (0,)), ((), ()))


def split(value):
    high = value.astype(jnp.bfloat16)
    low = (value - high.astype(jnp.float32)).astype(jnp.bfloat16)
    return high, low


def constants_kernel(fock_tiles, over_tiles, fock, over, fock_left, over_left, over_right):
    size = fock.shape[0]
    tiles = fock_tiles.shape[0]
    tile = size // tiles
    for a in range(tiles):
        for b in range(tiles):
            rows, cols = pl.ds(a * tile, tile), pl.ds(b * tile, tile)
            high, low = split(fock[rows, cols] * fock_tiles[a, b].astype(jnp.float32))
            for part, value in enumerate((high, high, low)):
                fock_left[rows, pl.ds(part * size + b * tile, tile)] = value
            high, low = split(over[rows, cols] * over_tiles[a, b].astype(jnp.float32))
            for part, value in enumerate((high, high, low)):
                over_left[rows, pl.ds(part * size + b * tile, tile)] = value
            for part, value in enumerate((high, high, low)):
                over_right[pl.ds(part * size + a * tile, tile), cols] = value


PIECE = 16


def pieces(size, begin=0):
    return [pl.ds(begin + n * PIECE, PIECE) for n in range(size // PIECE)]


def three_pass(wide, tall, left):
    size = min(wide.shape[1], tall.shape[0]) // 2
    first = DOT(wide[:, pl.ds(0, 2 * size)], tall[pl.ds(0, 2 * size), :], MATMUL)
    if left:
        return first + DOT(wide[:, pl.ds(2 * size, size)], tall[pl.ds(0, size), :], MATMUL)
    return first + DOT(wide[:, pl.ds(0, size)], tall[pl.ds(2 * size, size), :], MATMUL)


def first_slot():
    i, j = lax.axis_index("row"), lax.axis_index("col") * 2
    return (i + (i > j).astype(jnp.int32)) % 2


def pick_kernel(blocks, out, sem, *, second):
    slot = 1 - first_slot() if second else first_slot()
    copy = pltpu.make_async_copy(blocks.at[slot], out, sem)
    copy.start()
    copy.wait()


def pick_masked_kernel(domain, blocks, out0, out1, sems):
    size = blocks.shape[1]
    tiles = domain.shape[1]
    tile = size // tiles
    first = first_slot()
    slots, outs = (first, 1 - first), (out0, out1)
    body = pl.ds(0, size)
    copies = [pltpu.make_async_copy(blocks.at[slots[s]], outs[s].at[body], sems.at[s]) for s in range(2)]
    for copy in copies:
        copy.start()
    top = lax.broadcasted_iota(jnp.int32, (PAD, tile), 0) == 0
    for s in range(2):
        for t in range(tiles):
            value = domain[slots[s], t].astype(jnp.float32)
            outs[s][pl.ds(size, PAD), pl.ds(t * tile, tile)] = jnp.where(top, value, 0.0)
    for copy in copies:
        copy.wait()


def couple(occ, pattern, i, k):
    return occ[i, k] * pattern[i, k].astype(jnp.float32)


def own_kernel(table, occ, pattern, x0, x1, fock_left, over_left, out, stack):
    size = x0.shape[0]
    for s, x in enumerate((x0, x1)):
        for part in pieces(size):
            high, low = split(x[part, :])
            stack[part, pl.ds(s * size, size)] = high
            stack[pl.ds(size + part.start, PIECE), pl.ds(s * size, size)] = low
    out[...] = three_pass(fock_left, stack, True)
    over_x = three_pass(over_left, stack, True)
    for s in range(2):
        i, cols = table[2 * s], pl.ds(s * size, size)
        out[:, cols] = out[:, cols] - couple(occ, pattern, i, i) * over_x[:, s * size : (s + 1) * size]


def scale_kernel(table, occ, e_col, e_row, scale):
    for s in range(2):
        i, j = table[2 * s], table[2 * s + 1]
        scale[s] = 1.0 / (e_col[...] + e_row[...] - occ[i, i] - occ[j, j])


def update_kernel(
    table, occ, pattern, x0, x1, r0, r1, r2, r3, own, over_left, over_right, scale, k0, k1,
    y0, y1, stack, left, half, g,
):
    size = x0.shape[0]
    halo, x, k, y = (r0, r1, r2, r3), (x0, x1), (k0, k1), (y0, y1)
    coefs = []
    for s in range(2):
        factors = [couple(occ, pattern, table[2 * s], jnp.maximum(table[place + 1], 0)) for place in (5 + 4 * s, 7 + 4 * s)]
        coefs.append([0.0] * len(halo))
        for place, factor in zip((5 + 4 * s, 7 + 4 * s), factors):
            for number in range(len(halo)):
                here = (table[place] == number) & (table[place + 1] >= 0)
                coefs[s][number] += jnp.where(here, factor, 0.0)
    for part in pieces(size):
        for s in range(2):
            value = 0.0
            for number, r in enumerate(halo):
                value += coefs[s][number] * r[part, :]
            high, low = split(value)
            stack[part, pl.ds(s * size, size)] = high
            stack[pl.ds(size + part.start, PIECE), pl.ds(s * size, size)] = low
    half[...] = three_pass(over_left, stack, True)
    for s in range(2):
        for part in pieces(size):
            cols = pl.ds(s * size, size)
            high, low = split(own[part, cols] - half[part, cols])
            rows_s = pl.ds(s * size + part.start, PIECE)
            left[rows_s, pl.ds(0, size)] = high
            left[rows_s, pl.ds(size, size)] = low
    g[...] = three_pass(left, over_right, False)
    other = 1 - table[4]
    tile = min(size, 128)
    for s in range(2):
        base = (other if s == 0 else 1 - other) * size
        mask = k[s][pl.ds(size, PAD), :]
        for a in range(0, size, tile):
            mask_rows = DOT(mask[:, a : a + tile], mask, (((0,), (0,)), ((), ())))
            for b in range(0, size, tile):
                rows_a, cols_b = pl.ds(a, tile), pl.ds(b, tile)
                mirror = g[pl.ds(pl.multiple_of(base + b, tile), tile), rows_a].T
                total = k[s][rows_a, cols_b] + g[pl.ds(s * size + a, tile), cols_b] + mirror
                factor = mask_rows[:, b : b + tile] * scale[s, rows_a, cols_b]
                y[s][rows_a, cols_b] = x[s][rows_a, cols_b] - factor * total


SMEM = functools.partial(pl.BlockSpec, memory_space=pltpu.SMEM)
VMEM = functools.partial(pl.BlockSpec, memory_space=pltpu.VMEM)
ANY = functools.partial(pl.BlockSpec, memory_space=pl.ANY)
LIMIT = pltpu.CompilerParams(vmem_limit_bytes=24 * 2**20)


def constants(fock_tiles, over_tiles, fock, over):
    size = fock.shape[0]
    wide = pltpu.VMEM((size, 3 * size), jnp.bfloat16)
    return pl.pallas_call(
        constants_kernel,
        compiler_params=LIMIT,
        in_specs=[SMEM(), SMEM(), VMEM(), VMEM()],
        out_specs=[VMEM()] * 3,
        out_shape=[wide, wide, pltpu.VMEM((3 * size, size), jnp.bfloat16)],
    )(fock_tiles, over_tiles, fock, over)


def pick(blocks, second):
    return pl.pallas_call(
        functools.partial(pick_kernel, second=second),
        compiler_params=LIMIT,
        in_specs=[ANY()],
        out_specs=VMEM(),
        out_shape=pltpu.VMEM(blocks.shape[1:], blocks.dtype),
        scratch_shapes=[pltpu.SemaphoreType.DMA],
    )(blocks)


def pick_masked(blocks, domain):
    size = blocks.shape[1]
    block = pltpu.VMEM((size + PAD, size), blocks.dtype)
    return pl.pallas_call(
        pick_masked_kernel,
        compiler_params=LIMIT,
        in_specs=[SMEM(), ANY()],
        out_specs=[VMEM()] * 2,
        out_shape=[block] * 2,
        scratch_shapes=[pltpu.SemaphoreType.DMA((2,))],
    )(domain, blocks)


def own_part(table, occ, pattern, x, fock_left, over_left):
    size = x[0].shape[0]
    return pl.pallas_call(
        own_kernel,
        compiler_params=LIMIT,
        in_specs=[SMEM()] * 3 + [VMEM()] * 4,
        out_specs=VMEM(),
        out_shape=pltpu.VMEM((size, 2 * size), jnp.float32),
        scratch_shapes=[pltpu.VMEM((2 * size, 2 * size), jnp.bfloat16)],
    )(table, occ, pattern, *x, fock_left, over_left)


def scale_part(table, occ, e_col, e_row):
    size = e_col.shape[0]
    return pl.pallas_call(
        scale_kernel,
        compiler_params=LIMIT,
        in_specs=[SMEM()] * 2 + [VMEM()] * 2,
        out_specs=VMEM(),
        out_shape=pltpu.VMEM((2, size, size), jnp.float32),
    )(table, occ, e_col, e_row)


def update(table, occ, pattern, x, halo, own, over_left, over_right, scale, k):
    size = x[0].shape[0]
    block = pltpu.VMEM((size, size), jnp.float32)
    return pl.pallas_call(
        update_kernel,
        compiler_params=LIMIT,
        in_specs=[SMEM()] * 3 + [VMEM()] * 12,
        out_specs=[VMEM()] * 2,
        out_shape=[block, block],
        scratch_shapes=[
            pltpu.VMEM((2 * size, 2 * size), jnp.bfloat16),
            pltpu.VMEM((2 * size, 2 * size), jnp.bfloat16),
            pltpu.VMEM((size, 2 * size), jnp.float32),
            pltpu.VMEM((2 * size, size), jnp.float32),
        ],
    )(table, occ, pattern, *x, *halo, own, over_left, over_right, scale, *k)


def send(value, moves):
    value = lax.ppermute(value, AXES, moves)
    return pltpu.with_memory_space_constraint(value, pltpu.VMEM)


def solution(mesh):
    def shards(amplitudes, exchange_ints, fock, over, occ, energy, fock_tiles, over_tiles, pattern, domain):
        count = occ.shape[0]
        assert amplitudes.shape[:2] == (1, 2)
        table, gather, halo = make_plan(mesh, count)
        device = lax.axis_index("row") * mesh.shape["col"] + lax.axis_index("col")
        table = lax.dynamic_index_in_dim(jnp.asarray(table), device, keepdims=False)
        straight = first_slot() == 0

        def by_slot(a, b):
            return jnp.where(straight, a, b), jnp.where(straight, b, a)

        own_x = [pick(amplitudes[0], False)]
        blocks, own_x[0] = lax.optimization_barrier((amplitudes, own_x[0]))
        own_x.append(pick(blocks[0], True))
        x = [send(own_x[n], gather[n]) for n in range(2)]
        integrals, own_x = lax.optimization_barrier((exchange_ints, own_x))
        own_k = pick_masked(integrals[0], domain[0])
        k = [send(own_k[n], gather[n]) for n in range(2)]
        scale = scale_part(table, occ, energy[:, None], energy[None, :])
        ready = (constants(fock_tiles, over_tiles, fock, over), scale, table)
        x[0], ready = lax.optimization_barrier((x[0], ready))
        (fock_left, over_left, over_right), scale, table = ready
        for _ in range(ITERS):
            nearby = [send(x[n // 2], moves) for n, moves in enumerate(halo)]
            own = own_part(table, occ, pattern, x, fock_left, over_left)
            x = update(table, occ, pattern, x, nearby, own, over_left, over_right, scale, k)
        back = [
            lax.ppermute(value, AXES, [(target, source) for source, target in moves])
            for value, moves in zip(x, gather)
        ]
        return jnp.stack(by_slot(*back))[None]

    blocks = P("row", "col", None, None)
    in_specs = (blocks, blocks, P(), P(), P(), P(), P(), P(), P(), P("row", "col", None))
    return jax.shard_map(shards, mesh=mesh, in_specs=in_specs, out_specs=blocks, check_vma=False)
```
